128 devices in a mesh: req: 64 (over y, z, x), tp: 2 (over core).
Axes of the slice: x: 4, y: 4, z: 4, core: 2. Of those that a mesh axis runs over, the one named last changes fastest.
Arguments:
- tokens: bfloat16 [12288, 1536], P('req', 'tp'), may hold values from -6 to 6
- video_lengths: int32 [5], replicated, may hold values from 1 to 7680, 12288 in all
- timestep: int32 [1], replicated, may hold values from 1 to 1000
- time_weight: float32 [256, 4608], replicated, may hold values from -0.375 to 0.375
- block_mod: float32 [3, 1536], replicated, may hold values from -3 to 3
- w_query: bfloat16 [1536, 1536], P(None, 'tp')
- w_key: bfloat16 [1536, 1536], P(None, 'tp')
- w_value: bfloat16 [1536, 1536], P(None, 'tp'), may hold values from -0.15625 to 0.15625
- w_out: bfloat16 [1536, 1536], P('tp'), may hold values from -0.15625 to 0.15625
Outputs:
- velocity: bfloat16 [12288, 1536], P('req', 'tp')
- stepped: bfloat16 [12288, 1536], P('req', 'tp')
The draws below stay inside these ranges and needn't reach their ends.
Inputs may be any that keep to these rules, and one draw needn't show every extreme that they name: `video_lengths`: the videos' lengths in packing order; they sum to 12288 and the longest has exactly 7680 tokens.
All inputs are finite; a program needn't handle non-finite values.
Results may differ from the reference program's by a relative error of at most 0.017.
Values may be sent and summed in bfloat16 or wider, within the bound.
A program may use at most 256 MiB of HBM per device.

```python
import math
import jax
import jax.numpy as jnp
import numpy as np
from jax import lax

HEADS = 12
HEAD_DIM = 128
FREQ = 256
D = 1536
VIDEOS = 5
STEPS = 1000
TOKENS = 12288
MOST = 7680


def paired_weights(seed_key):
    first = jax.random.normal(jax.random.fold_in(seed_key, 11), (D, D), jnp.float32)
    second = jax.random.normal(jax.random.fold_in(seed_key, 12), (D, D), jnp.float32)
    factor = 1.7 * D ** (-0.5)
    return (first * factor, second * factor)


def draw_w_query(key, part):
    return paired_weights(key)[0].astype(jnp.bfloat16)


def draw_w_key(key, part):
    return paired_weights(key)[1].astype(jnp.bfloat16)


def block_levels(stream_key, extent, shards, smallest, largest):
    level, own = 1.0, jax.random.fold_in(stream_key, 6)
    for position, parts in shards:
        draws = jnp.exp(jax.random.uniform(jax.random.fold_in(own, position), (parts,), jnp.float32, smallest / len(shards), largest / len(shards)))
        level = level * jnp.repeat(draws, extent[position] // parts).reshape([-1 if axis == position else 1 for axis in range(len(extent))])
    return level


def split_up(number_of, total, most, slope):
    loads = [(1 << 20) // math.isqrt(standing ** slope) + 1 for standing in range(2, number_of + 1)]
    surplus, given = total - most - (number_of - 1), [1] * (number_of - 1)
    while surplus > 0:
        movable = [i for i in range(number_of - 1) if given[i] < most]
        whole, remaining = sum([loads[i] for i in movable]), surplus
        for i in movable:
            extra = min(most - given[i], max(1, remaining * loads[i] // whole), surplus)
            given[i] = given[i] + extra
            surplus = surplus - extra
    return np.array([most] + given)


def ragged(stream_key, number_of, total, bound, skew):
    if number_of == 2:
        one = jax.random.randint(stream_key, (), max(1, total - bound), min(bound, total - 1) + 1)
        return jnp.stack([one, total - one])
    sizes = jnp.asarray(split_up(number_of, total, bound, skew), jnp.int32)
    couples = (number_of - 1) // 2
    donor, taker = sizes[1:1 + 2 * couples:2], sizes[2:2 + 2 * couples:2]
    room = jnp.minimum(donor - 1, bound - taker)
    moved = jax.random.randint(jax.random.fold_in(stream_key, 1), (couples,), 0, 1 << 20) % (room + 1)
    sizes = sizes.at[1:1 + 2 * couples:2].set(donor - moved).at[2:2 + 2 * couples:2].set(taker + moved)
    return sizes[jax.random.permutation(jax.random.fold_in(stream_key, 2), number_of)]


def scatter_about(rng, extent, width, most, shards=(), kind=jnp.bfloat16):
    result = jax.random.normal(rng, extent, jnp.float32) * width
    if len(shards) > 0:
        result = block_levels(rng, extent, shards, -0.22, 0.18) * result
    return jnp.clip(result, min=-most, max=most).astype(kind)


def setup_inputs(seed: int = 0) -> dict:
    arg_keys = jax.random.split(jax.random.key(seed), 10)
    return {
        "tokens": scatter_about(arg_keys[0], (TOKENS, D), 1.0, 6.0, ((0, 64), (1, 2))),
        "video_lengths": ragged(arg_keys[1], VIDEOS, TOKENS, MOST, 2).astype(jnp.int32),
        "timestep": jax.random.randint(arg_keys[2], (1,), 1, STEPS + 1).astype(jnp.int32),
        "time_weight": scatter_about(arg_keys[3], (FREQ, 3 * D), FREQ ** -0.5, 0.375, (), jnp.float32),
        "block_mod": scatter_about(arg_keys[4], (3, D), 0.5, 3.0, (), jnp.float32),
        "w_query": draw_w_query(jax.random.fold_in(arg_keys[9], 71), 0),
        "w_key": draw_w_key(jax.random.fold_in(arg_keys[9], 71), 0),
        "w_value": scatter_about(arg_keys[7], (D, D), D ** -0.5, 0.15625, ((1, 2),)),
        "w_out": scatter_about(arg_keys[8], (D, D), D ** -0.5, 0.15625, ((0, 2),)),
    }


def noise_level(step_value):
    frac = step_value / STEPS
    return 5.0 * frac / (1.0 + 4.0 * frac)

def reference(tokens, video_lengths, timestep, time_weight, block_mod, w_query, w_key, w_value, w_out):
    time_value = timestep[0].astype(jnp.float32)
    sigma = noise_level(time_value)
    delta_sigma = noise_level(time_value - 1.0) - sigma
    half_freq = FREQ // 2
    frequency = jnp.exp(-math.log(10000.0) * jnp.arange(half_freq, dtype=jnp.float32) / half_freq)
    angle = 1000.0 * sigma * frequency
    embedding = jnp.concatenate([jnp.cos(angle), jnp.sin(angle)])
    modulation = jnp.dot(jax.nn.silu(embedding)[None, :], time_weight, precision=lax.Precision.HIGHEST, preferred_element_type=jnp.float32)[0]
    modulation = modulation.reshape(3, D) + block_mod
    shift, scale, gate = (modulation[0], modulation[1], modulation[2])
    residual = tokens.astype(jnp.float32)
    mean = lax.optimization_barrier(jnp.mean(residual, axis=1, keepdims=True))
    centred = residual - mean
    variance = lax.optimization_barrier(jnp.mean(centred * centred, axis=1, keepdims=True))
    normed = (centred * lax.rsqrt(variance + 1e-06) * (1.0 + scale) + shift).astype(jnp.bfloat16)
    query = jnp.dot(normed, w_query, preferred_element_type=jnp.float32).astype(jnp.bfloat16)
    keys = jnp.dot(normed, w_key, preferred_element_type=jnp.float32).astype(jnp.bfloat16)
    values = jnp.dot(normed, w_value, preferred_element_type=jnp.float32).astype(jnp.bfloat16)
    video_ends = jnp.cumsum(video_lengths).astype(jnp.int32)
    token_index = jnp.arange(TOKENS, dtype=jnp.int32)
    video_of = lax.optimization_barrier(jnp.sum((token_index[:, None] >= video_ends[None, :]).astype(jnp.int32), axis=1))
    same_video = video_of[:, None] == video_of[None, :]

    def split_heads(array):
        return jnp.transpose(array.reshape(TOKENS, HEADS, HEAD_DIM), (1, 0, 2))

    def one_head(packed):
        query_head, key_head, value_head = packed
        scores = jnp.dot(query_head, key_head.T, preferred_element_type=jnp.float32) / math.sqrt(HEAD_DIM)
        scores = jnp.where(same_video, scores, -1e+30)
        row_max = lax.optimization_barrier(jnp.max(scores, axis=1, keepdims=True))
        probs = jnp.where(same_video, jnp.exp(scores - row_max), 0.0)
        row_sum = lax.optimization_barrier(jnp.sum(probs, axis=1, keepdims=True))
        weighted = jnp.dot(probs.astype(jnp.bfloat16), value_head, preferred_element_type=jnp.float32)
        return (weighted / row_sum).astype(jnp.bfloat16)
    attended = lax.map(one_head, (split_heads(query), split_heads(keys), split_heads(values)))
    attended = jnp.transpose(attended, (1, 0, 2)).reshape(TOKENS, D)
    projected = jnp.dot(attended, w_out, preferred_element_type=jnp.float32)
    branch = gate * projected
    velocity = branch.astype(jnp.bfloat16)
    stepped = (residual + delta_sigma * branch).astype(jnp.bfloat16)
    return (velocity, stepped)
```

```python
import math

import jax
import jax.numpy as jnp
from jax import lax
from jax.sharding import PartitionSpec as P

HEAD_DIM = 128
STEPS = 1000


def noise_level(step_value):
    frac = step_value / STEPS
    return 5.0 * frac / (1.0 + 4.0 * frac)


def on_device(
    tokens, video_lengths, timestep, time_weight, block_mod, w_query, w_key, w_value, w_out
):
    tok_rows = tokens.shape[0]
    width = time_weight.shape[1] // 3
    full_rows = lax.all_gather(tokens, "tp", axis=1, tiled=True)
    time_value = timestep[0].astype(jnp.float32)
    sigma = noise_level(time_value)
    delta_sigma = noise_level(time_value - 1.0) - sigma
    half_freq = time_weight.shape[0] // 2
    frequency = jnp.exp(-math.log(10000.0) * jnp.arange(half_freq, dtype=jnp.float32) / half_freq)
    angle = 1000.0 * sigma * frequency
    embedding = jnp.concatenate([jnp.cos(angle), jnp.sin(angle)])
    modulation = jnp.dot(
        jax.nn.silu(embedding)[None, :],
        time_weight,
        precision=lax.Precision.HIGHEST,
        preferred_element_type=jnp.float32,
    )[0]
    modulation = modulation.reshape(3, width) + block_mod
    shift, scale, gate = (modulation[0], modulation[1], modulation[2])
    as_float = full_rows.astype(jnp.float32)
    mean = jnp.mean(as_float, axis=1, keepdims=True)
    centred = as_float - mean
    variance = jnp.mean(centred * centred, axis=1, keepdims=True)
    normed = (centred * lax.rsqrt(variance + 1e-06) * (1.0 + scale) + shift).astype(jnp.bfloat16)
    query = jnp.dot(normed, w_query, preferred_element_type=jnp.float32).astype(jnp.bfloat16)
    keys = jnp.dot(normed, w_key, preferred_element_type=jnp.float32).astype(jnp.bfloat16)
    values = jnp.dot(normed, w_value, preferred_element_type=jnp.float32).astype(jnp.bfloat16)
    heads_here = query.shape[1] // HEAD_DIM
    query_heads = query.reshape(tok_rows, heads_here, HEAD_DIM)
    start_row = lax.axis_index("req") * tok_rows
    query_index = start_row + jnp.arange(tok_rows, dtype=jnp.int32)
    video_ends = jnp.cumsum(video_lengths)
    video_starts = video_ends - video_lengths
    inside = jnp.logical_and(
        query_index[:, None] >= video_starts[None, :], query_index[:, None] < video_ends[None, :]
    )
    query_low = jnp.sum(jnp.where(inside, video_starts[None, :], 0), axis=1)
    query_high = jnp.sum(jnp.where(inside, video_ends[None, :], 0), axis=1)
    key_index = jnp.arange(tok_rows * lax.psum(1, "req"), dtype=jnp.int32)
    valid = jnp.logical_and(
        key_index[None, :] >= query_low[:, None], key_index[None, :] < query_high[:, None]
    )
    outputs = []
    for head in range(heads_here):
        cols = slice(head * HEAD_DIM, (head + 1) * HEAD_DIM)
        packed = jnp.concatenate([keys[:, cols], values[:, cols]], axis=1)
        gathered = lax.all_gather(packed, "req", axis=0, tiled=True)
        key_head = gathered[:, :HEAD_DIM]
        value_head = gathered[:, HEAD_DIM:]
        scores = jnp.dot(
            query[:, cols], key_head.T, preferred_element_type=jnp.float32
        ) / math.sqrt(HEAD_DIM)
        row_max = jnp.max(jnp.where(valid, scores, -1e30), axis=1, keepdims=True)
        probs = jnp.where(valid, jnp.exp(scores - row_max), 0.0)
        row_sum = jnp.sum(probs, axis=1, keepdims=True)
        weighted = jnp.dot(
            probs.astype(jnp.bfloat16), value_head, preferred_element_type=jnp.float32
        )
        outputs.append((weighted / row_sum).astype(jnp.bfloat16))
    attended = jnp.concatenate(outputs, axis=1)
    partial_value = jnp.dot(attended, w_out, preferred_element_type=jnp.float32)
    own_sum = lax.psum_scatter(
        partial_value.astype(jnp.bfloat16), "tp", scatter_dimension=1, tiled=True
    ).astype(jnp.float32)
    share = own_sum.shape[1]
    gate_share = lax.dynamic_slice_in_dim(gate, lax.axis_index("tp") * share, share)
    branch = gate_share[None, :] * own_sum
    velocity = branch.astype(jnp.bfloat16)
    stepped = (tokens.astype(jnp.float32) + delta_sigma * branch).astype(jnp.bfloat16)
    return (velocity, stepped)


def solution(mesh):
    return jax.shard_map(
        on_device,
        mesh=mesh,
        in_specs=(
            P("req", "tp"),
            P(),
            P(),
            P(),
            P(),
            P(None, "tp"),
            P(None, "tp"),
            P(None, "tp"),
            P("tp", None),
        ),
        out_specs=(P("req", "tp"), P("req", "tp")),
        check_vma=False,
    )
```

```python
import math

import jax
import jax.numpy as jnp
from jax import lax
from jax.sharding import PartitionSpec as P

HEAD_DIM = 128
STEPS = 1000


def noise_level(step_value):
    frac = step_value / STEPS
    return 5.0 * frac / (1.0 + 4.0 * frac)


def on_device(
    tokens, video_lengths, timestep, time_weight, block_mod, w_query, w_key, w_value, w_out
):
    tok_rows = tokens.shape[0]
    width = time_weight.shape[1] // 3
    full_rows = lax.all_gather(tokens, "tp", axis=1, tiled=True)
    time_value = timestep[0].astype(jnp.float32)
    sigma = noise_level(time_value)
    delta_sigma = noise_level(time_value - 1.0) - sigma
    half_freq = time_weight.shape[0] // 2
    frequency = jnp.exp(-math.log(10000.0) * jnp.arange(half_freq, dtype=jnp.float32) / half_freq)
    angle = 1000.0 * sigma * frequency
    embedding = jnp.concatenate([jnp.cos(angle), jnp.sin(angle)])
    modulation = jnp.dot(
        jax.nn.silu(embedding)[None, :],
        time_weight,
        precision=lax.Precision.HIGHEST,
        preferred_element_type=jnp.float32,
    )[0]
    modulation = modulation.reshape(3, width) + block_mod
    shift, scale, gate = (modulation[0], modulation[1], modulation[2])
    as_float = full_rows.astype(jnp.float32)
    mean = jnp.mean(as_float, axis=1, keepdims=True)
    centred = as_float - mean
    variance = jnp.mean(centred * centred, axis=1, keepdims=True)
    normed = (centred * lax.rsqrt(variance + 1e-06) * (1.0 + scale) + shift).astype(jnp.bfloat16)
    query = jnp.dot(normed, w_query, preferred_element_type=jnp.float32).astype(jnp.bfloat16)
    keys = jnp.dot(normed, w_key, preferred_element_type=jnp.float32).astype(jnp.bfloat16)
    values = jnp.dot(normed, w_value, preferred_element_type=jnp.float32).astype(jnp.bfloat16)
    heads_here = query.shape[1] // HEAD_DIM
    query_heads = query.reshape(tok_rows, heads_here, HEAD_DIM)
    start_row = lax.axis_index("req") * tok_rows
    query_index = start_row + jnp.arange(tok_rows, dtype=jnp.int32)
    video_ends = jnp.cumsum(video_lengths)
    video_starts = video_ends - video_lengths
    inside = jnp.logical_and(
        query_index[:, None] >= video_starts[None, :], query_index[:, None] < video_ends[None, :]
    )
    query_low = jnp.sum(jnp.where(inside, video_starts[None, :], 0), axis=1)
    query_high = jnp.sum(jnp.where(inside, video_ends[None, :], 0), axis=1)
    span_low = jnp.min(query_low)
    span_high = jnp.max(query_high)

    def score_block(carry, pieces):
        row_max, row_sum, weighted = carry
        key_piece, value_piece = pieces
        count = key_piece.shape[0]
        key_heads = key_piece.reshape(count, heads_here, HEAD_DIM)
        value_heads = value_piece.reshape(count, heads_here, HEAD_DIM)
        scores = jnp.einsum(
            "qhd,khd->hqk", query_heads, key_heads, preferred_element_type=jnp.float32
        ) / math.sqrt(HEAD_DIM)
        key_index = jnp.arange(count, dtype=jnp.int32)
        valid = jnp.logical_and(
            key_index[None, :] >= query_low[:, None], key_index[None, :] < query_high[:, None]
        )[None, :, :]
        block_max = jnp.max(jnp.where(valid, scores, -1e30), axis=2)
        new_max = jnp.maximum(row_max, block_max)
        probs = jnp.where(valid, jnp.exp(scores - new_max[:, :, None]), 0.0)
        new_sum = jnp.sum(probs, axis=2)
        update = jnp.einsum(
            "hqk,khd->hqd",
            probs.astype(jnp.bfloat16),
            value_heads,
            preferred_element_type=jnp.float32,
        )
        return (new_max, new_sum, update)

    initial = (
        jnp.full((heads_here, tok_rows), -1e30, jnp.float32),
        jnp.zeros((heads_here, tok_rows), jnp.float32),
        jnp.zeros((heads_here, tok_rows, HEAD_DIM), jnp.float32),
    )
    gathered = lax.all_gather(jnp.concatenate([keys, values], axis=1), "req", axis=0, tiled=True)
    pieces = (gathered[:, : keys.shape[1]], gathered[:, keys.shape[1] :])
    start = jnp.int32(0)
    count = pieces[0].shape[0]
    touches = jnp.logical_and(start < span_high, start + count > span_low)
    carry = lax.cond(
        touches, lambda state: score_block(state, pieces), lambda state: state, initial
    )
    row_max, row_sum, weighted = carry
    attended = (weighted / row_sum[:, :, None]).astype(jnp.bfloat16)
    attended = jnp.transpose(attended, (1, 0, 2)).reshape(tok_rows, heads_here * HEAD_DIM)
    partial_value = jnp.dot(attended, w_out, preferred_element_type=jnp.float32)
    own_sum = lax.psum_scatter(
        partial_value.astype(jnp.bfloat16), "tp", scatter_dimension=1, tiled=True
    ).astype(jnp.float32)
    share = own_sum.shape[1]
    gate_share = lax.dynamic_slice_in_dim(gate, lax.axis_index("tp") * share, share)
    branch = gate_share[None, :] * own_sum
    velocity = branch.astype(jnp.bfloat16)
    stepped = (tokens.astype(jnp.float32) + delta_sigma * branch).astype(jnp.bfloat16)
    return (velocity, stepped)


def solution(mesh):
    return jax.shard_map(
        on_device,
        mesh=mesh,
        in_specs=(
            P("req", "tp"),
            P(),
            P(),
            P(),
            P(),
            P(None, "tp"),
            P(None, "tp"),
            P(None, "tp"),
            P("tp", None),
        ),
        out_specs=(P("req", "tp"), P("req", "tp")),
        check_vma=False,
    )
```

```python
import math

import jax
import jax.numpy as jnp
from jax import lax
from jax.experimental import pallas as pl
from jax.experimental.pallas import tpu as pltpu
from jax.sharding import PartitionSpec as P

HEAD_DIM = 128
STEPS = 1000
KEY_BLOCK = 1024


def noise_level(step_value):
    frac = step_value / STEPS
    return 5.0 * frac / (1.0 + 4.0 * frac)


def attention_kernel(span_ref, query_ref, key_ref, value_ref, low_ref, high_ref, out_ref,
                     max_ref, sum_ref, acc_ref):
    block = pl.program_id(0)
    heads = query_ref.shape[1] // HEAD_DIM
    first = span_ref[0] // KEY_BLOCK
    last = (span_ref[1] - 1) // KEY_BLOCK

    @pl.when(block == 0)
    def _():
        max_ref[...] = jnp.full(max_ref.shape, -1e30, jnp.float32)
        sum_ref[...] = jnp.zeros(sum_ref.shape, jnp.float32)
        acc_ref[...] = jnp.zeros(acc_ref.shape, jnp.float32)

    @pl.when(jnp.logical_and(block >= first, block <= last))
    def _():
        rows = query_ref.shape[0]
        key_index = block * KEY_BLOCK + lax.broadcasted_iota(jnp.int32, (rows, KEY_BLOCK), 1)
        valid = jnp.logical_and(key_index >= low_ref[...], key_index < high_ref[...])
        for head in range(heads):
            cols = slice(head * HEAD_DIM, (head + 1) * HEAD_DIM)
            scores = lax.dot_general(
                query_ref[:, cols], key_ref[:, cols], (((1,), (1,)), ((), ())),
                preferred_element_type=jnp.float32,
            ) * (1.0 / math.sqrt(HEAD_DIM))
            old_max = max_ref[head]
            new_max = jnp.maximum(
                old_max, jnp.max(jnp.where(valid, scores, -1e30), axis=1, keepdims=True)
            )
            probs = jnp.where(valid, jnp.exp(scores - new_max), 0.0)
            alpha = jnp.exp(old_max - new_max)
            sum_ref[head] = alpha * sum_ref[head] + jnp.sum(probs, axis=1, keepdims=True)
            acc_ref[:, cols] = alpha * acc_ref[:, cols] + jnp.dot(
                probs.astype(jnp.bfloat16), value_ref[:, cols],
                preferred_element_type=jnp.float32,
            )
            max_ref[head] = new_max

    @pl.when(block == pl.num_programs(0) - 1)
    def _():
        for head in range(heads):
            cols = slice(head * HEAD_DIM, (head + 1) * HEAD_DIM)
            out_ref[:, cols] = (acc_ref[:, cols] / sum_ref[head]).astype(out_ref.dtype)


def attention(span, query, packed, query_low, query_high):
    rows, width = query.shape
    blocks = packed.shape[0] // KEY_BLOCK

    def key_map(block, span_ref):
        first = span_ref[0] // KEY_BLOCK
        last = (span_ref[1] - 1) // KEY_BLOCK
        return (jnp.minimum(jnp.maximum(block, first), last), 0)

    def value_map(block, span_ref):
        first = span_ref[0] // KEY_BLOCK
        last = (span_ref[1] - 1) // KEY_BLOCK
        return (jnp.minimum(jnp.maximum(block, first), last), 1)

    whole = lambda block, span_ref: (0, 0)
    heads = width // HEAD_DIM
    return pl.pallas_call(
        attention_kernel,
        grid_spec=pltpu.PrefetchScalarGridSpec(
            num_scalar_prefetch=1,
            grid=(blocks,),
            in_specs=[
                pl.BlockSpec((rows, width), whole),
                pl.BlockSpec((KEY_BLOCK, width), key_map),
                pl.BlockSpec((KEY_BLOCK, width), value_map),
                pl.BlockSpec((rows, 1), whole),
                pl.BlockSpec((rows, 1), whole),
            ],
            out_specs=pl.BlockSpec((rows, width), whole),
            scratch_shapes=[
                pltpu.VMEM((heads, rows, 1), jnp.float32),
                pltpu.VMEM((heads, rows, 1), jnp.float32),
                pltpu.VMEM((rows, width), jnp.float32),
            ],
        ),
        out_shape=jax.ShapeDtypeStruct((rows, width), jnp.bfloat16),
    )(span, query, packed, packed, query_low, query_high)


def on_device(
    tokens, video_lengths, timestep, time_weight, block_mod, w_query, w_key, w_value, w_out
):
    tok_rows = tokens.shape[0]
    width = time_weight.shape[1] // 3
    full_rows = lax.all_gather(tokens, "tp", axis=1, tiled=True)
    time_value = timestep[0].astype(jnp.float32)
    sigma = noise_level(time_value)
    delta_sigma = noise_level(time_value - 1.0) - sigma
    half_freq = time_weight.shape[0] // 2
    frequency = jnp.exp(-math.log(10000.0) * jnp.arange(half_freq, dtype=jnp.float32) / half_freq)
    angle = 1000.0 * sigma * frequency
    embedding = jnp.concatenate([jnp.cos(angle), jnp.sin(angle)])
    modulation = jnp.dot(
        jax.nn.silu(embedding)[None, :],
        time_weight,
        precision=lax.Precision.HIGHEST,
        preferred_element_type=jnp.float32,
    )[0]
    modulation = modulation.reshape(3, width) + block_mod
    shift, scale, gate = (modulation[0], modulation[1], modulation[2])
    as_float = full_rows.astype(jnp.float32)
    mean = jnp.mean(as_float, axis=1, keepdims=True)
    centred = as_float - mean
    variance = jnp.mean(centred * centred, axis=1, keepdims=True)
    normed = (centred * lax.rsqrt(variance + 1e-06) * (1.0 + scale) + shift).astype(jnp.bfloat16)
    query = jnp.dot(normed, w_query, preferred_element_type=jnp.float32).astype(jnp.bfloat16)
    keys = jnp.dot(normed, w_key, preferred_element_type=jnp.float32).astype(jnp.bfloat16)
    values = jnp.dot(normed, w_value, preferred_element_type=jnp.float32).astype(jnp.bfloat16)
    start_row = lax.axis_index("req") * tok_rows
    query_index = start_row + jnp.arange(tok_rows, dtype=jnp.int32)
    video_ends = jnp.cumsum(video_lengths)
    video_starts = video_ends - video_lengths
    inside = jnp.logical_and(
        query_index[:, None] >= video_starts[None, :], query_index[:, None] < video_ends[None, :]
    )
    query_low = jnp.sum(jnp.where(inside, video_starts[None, :], 0), axis=1)
    query_high = jnp.sum(jnp.where(inside, video_ends[None, :], 0), axis=1)
    span = jnp.stack([jnp.min(query_low), jnp.max(query_high)]).astype(jnp.int32)
    packed = lax.all_gather(jnp.concatenate([keys, values], axis=1), "req", axis=0, tiled=True)
    attended = attention(span, query, packed, query_low[:, None], query_high[:, None])
    partial_value = jnp.dot(attended, w_out, preferred_element_type=jnp.float32)
    own_sum = lax.psum_scatter(
        partial_value.astype(jnp.bfloat16), "tp", scatter_dimension=1, tiled=True
    ).astype(jnp.float32)
    share = own_sum.shape[1]
    gate_share = lax.dynamic_slice_in_dim(gate, lax.axis_index("tp") * share, share)
    branch = gate_share[None, :] * own_sum
    velocity = branch.astype(jnp.bfloat16)
    stepped = (tokens.astype(jnp.float32) + delta_sigma * branch).astype(jnp.bfloat16)
    return (velocity, stepped)


def solution(mesh):
    return jax.shard_map(
        on_device,
        mesh=mesh,
        in_specs=(
            P("req", "tp"),
            P(),
            P(),
            P(),
            P(),
            P(None, "tp"),
            P(None, "tp"),
            P(None, "tp"),
            P("tp", None),
        ),
        out_specs=(P("req", "tp"), P("req", "tp")),
        check_vma=False,
    )
```

```python
import math

import jax
import jax.numpy as jnp
from jax import lax
from jax.experimental import pallas as pl
from jax.experimental.pallas import tpu as pltpu
from jax.sharding import PartitionSpec as P

HEAD_DIM = 128
STEPS = 1000
KEY_BLOCK = 1024


def noise_level(step_value):
    frac = step_value / STEPS
    return 5.0 * frac / (1.0 + 4.0 * frac)


def attention_kernel(span_ref, query_ref, key_ref, value_ref, low_ref, high_ref, out_ref,
                     max_ref, sum_ref, acc_ref):
    block = pl.program_id(0)
    heads = query_ref.shape[1] // HEAD_DIM
    first = span_ref[0] // KEY_BLOCK
    last = (span_ref[1] - 1) // KEY_BLOCK

    @pl.when(block == 0)
    def _():
        max_ref[...] = jnp.full(max_ref.shape, -1e30, jnp.float32)
        sum_ref[...] = jnp.zeros(sum_ref.shape, jnp.float32)
        acc_ref[...] = jnp.zeros(acc_ref.shape, jnp.float32)

    @pl.when(jnp.logical_and(block >= first, block <= last))
    def _():
        rows = query_ref.shape[0]
        key_index = block * KEY_BLOCK + lax.broadcasted_iota(jnp.int32, (rows, KEY_BLOCK), 1)
        valid = jnp.logical_and(key_index >= low_ref[...], key_index < high_ref[...])
        for head in range(heads):
            cols = slice(head * HEAD_DIM, (head + 1) * HEAD_DIM)
            scores = lax.dot_general(
                query_ref[:, cols], key_ref[:, cols], (((1,), (1,)), ((), ())),
                preferred_element_type=jnp.float32,
            ) * (1.0 / math.sqrt(HEAD_DIM))
            old_max = max_ref[head]
            new_max = jnp.maximum(
                old_max, jnp.max(jnp.where(valid, scores, -1e30), axis=1, keepdims=True)
            )
            probs = jnp.where(valid, jnp.exp(scores - new_max), 0.0)
            alpha = jnp.exp(old_max - new_max)
            sum_ref[head] = alpha * sum_ref[head] + jnp.sum(probs, axis=1, keepdims=True)
            acc_ref[:, cols] = alpha * acc_ref[:, cols] + jnp.dot(
                probs.astype(jnp.bfloat16), value_ref[:, cols],
                preferred_element_type=jnp.float32,
            )
            max_ref[head] = new_max

    @pl.when(block == pl.num_programs(0) - 1)
    def _():
        for head in range(heads):
            cols = slice(head * HEAD_DIM, (head + 1) * HEAD_DIM)
            out_ref[:, cols] = (acc_ref[:, cols] / sum_ref[head]).astype(out_ref.dtype)


def attention(span, query, packed, query_low, query_high):
    rows, width = query.shape
    blocks = packed.shape[0] // KEY_BLOCK

    def key_map(block, span_ref):
        first = span_ref[0] // KEY_BLOCK
        last = (span_ref[1] - 1) // KEY_BLOCK
        return (jnp.minimum(jnp.maximum(block, first), last), 0)

    def value_map(block, span_ref):
        first = span_ref[0] // KEY_BLOCK
        last = (span_ref[1] - 1) // KEY_BLOCK
        return (jnp.minimum(jnp.maximum(block, first), last), 1)

    whole = lambda block, span_ref: (0, 0)
    heads = width // HEAD_DIM
    return pl.pallas_call(
        attention_kernel,
        grid_spec=pltpu.PrefetchScalarGridSpec(
            num_scalar_prefetch=1,
            grid=(blocks,),
            in_specs=[
                pl.BlockSpec((rows, width), whole),
                pl.BlockSpec((KEY_BLOCK, width), key_map),
                pl.BlockSpec((KEY_BLOCK, width), value_map),
                pl.BlockSpec((rows, 1), whole),
                pl.BlockSpec((rows, 1), whole),
            ],
            out_specs=pl.BlockSpec((rows, width), whole),
            scratch_shapes=[
                pltpu.VMEM((heads, rows, 1), jnp.float32),
                pltpu.VMEM((heads, rows, 1), jnp.float32),
                pltpu.VMEM((rows, width), jnp.float32),
            ],
        ),
        out_shape=jax.ShapeDtypeStruct((rows, width), jnp.bfloat16),
    )(span, query, packed, packed, query_low, query_high)


def on_device(
    tokens, video_lengths, timestep, time_weight, block_mod, w_query, w_key, w_value, w_out
):
    tok_rows = tokens.shape[0]
    width = time_weight.shape[1] // 3
    full_rows = lax.all_gather(tokens, "tp", axis=1, tiled=True)
    time_value = timestep[0].astype(jnp.float32)
    sigma = noise_level(time_value)
    delta_sigma = noise_level(time_value - 1.0) - sigma
    half_freq = time_weight.shape[0] // 2
    frequency = jnp.exp(-math.log(10000.0) * jnp.arange(half_freq, dtype=jnp.float32) / half_freq)
    angle = 1000.0 * sigma * frequency
    embedding = jnp.concatenate([jnp.cos(angle), jnp.sin(angle)])
    modulation = jnp.dot(
        jax.nn.silu(embedding)[None, :],
        time_weight,
        precision=lax.Precision.HIGHEST,
        preferred_element_type=jnp.float32,
    )[0]
    modulation = modulation.reshape(3, width) + block_mod
    shift, scale, gate = (modulation[0], modulation[1], modulation[2])
    as_float = full_rows.astype(jnp.float32)
    mean = jnp.mean(as_float, axis=1, keepdims=True)
    centred = as_float - mean
    variance = jnp.mean(centred * centred, axis=1, keepdims=True)
    normed = (centred * lax.rsqrt(variance + 1e-06) * (1.0 + scale) + shift).astype(jnp.bfloat16)
    query = jnp.dot(normed, w_query, preferred_element_type=jnp.float32).astype(jnp.bfloat16)
    keys = jnp.dot(normed, w_key, preferred_element_type=jnp.float32).astype(jnp.bfloat16)
    values = jnp.dot(normed, w_value, preferred_element_type=jnp.float32).astype(jnp.bfloat16)
    group_width = query.shape[1] // 2
    groups = []
    for group in range(2):
        cols = slice(group * group_width, (group + 1) * group_width)
        groups.append(jnp.concatenate([keys[:, cols], values[:, cols], query[:, cols]], axis=1))
    swapped = lax.all_to_all(
        jnp.concatenate(groups, axis=0), "pair", split_axis=0, concat_axis=0, tiled=True
    )
    pair_rows = swapped.shape[0]
    kv_local = swapped[:, : 2 * group_width]
    query_local = swapped[:, 2 * group_width :]
    start_row = lax.axis_index("r") * pair_rows
    query_index = start_row + jnp.arange(pair_rows, dtype=jnp.int32)
    video_ends = jnp.cumsum(video_lengths)
    video_starts = video_ends - video_lengths
    inside = jnp.logical_and(
        query_index[:, None] >= video_starts[None, :], query_index[:, None] < video_ends[None, :]
    )
    query_low = jnp.sum(jnp.where(inside, video_starts[None, :], 0), axis=1)
    query_high = jnp.sum(jnp.where(inside, video_ends[None, :], 0), axis=1)
    span = jnp.stack([jnp.min(query_low), jnp.max(query_high)]).astype(jnp.int32)
    packed = lax.all_gather(kv_local, "r", axis=0, tiled=True)
    attended_local = attention(span, query_local, packed, query_low[:, None], query_high[:, None])
    attended = lax.all_to_all(attended_local, "pair", split_axis=0, concat_axis=1, tiled=True)
    partial_value = jnp.dot(attended, w_out, preferred_element_type=jnp.float32)
    own_sum = lax.psum_scatter(
        partial_value.astype(jnp.bfloat16), "tp", scatter_dimension=1, tiled=True
    ).astype(jnp.float32)
    share = own_sum.shape[1]
    gate_share = lax.dynamic_slice_in_dim(gate, lax.axis_index("tp") * share, share)
    branch = gate_share[None, :] * own_sum
    velocity = branch.astype(jnp.bfloat16)
    stepped = (tokens.astype(jnp.float32) + delta_sigma * branch).astype(jnp.bfloat16)
    return (velocity, stepped)


def solution(mesh):
    req_size, tp_size = mesh.devices.shape
    split_mesh = jax.sharding.Mesh(
        mesh.devices.reshape(req_size // 2, 2, tp_size), ("r", "pair", "tp")
    )
    rows = ("r", "pair")
    return jax.shard_map(
        on_device,
        mesh=split_mesh,
        in_specs=(
            P(rows, "tp"),
            P(),
            P(),
            P(),
            P(),
            P(None, "tp"),
            P(None, "tp"),
            P(None, "tp"),
            P("tp", None),
        ),
        out_specs=(P(rows, "tp"), P(rows, "tp")),
        check_vma=False,
    )
```

```python
import math

import jax
import jax.numpy as jnp
from jax import lax
from jax.experimental import pallas as pl
from jax.experimental.pallas import tpu as pltpu
from jax.sharding import PartitionSpec as P

HEAD_DIM = 128
STEPS = 1000
KEY_BLOCK = 1024
EXP2_SCALE = math.log2(math.e) / math.sqrt(HEAD_DIM)


def noise_level(step_value):
    frac = step_value / STEPS
    return 5.0 * frac / (1.0 + 4.0 * frac)


def attention_kernel(span_ref, query_ref, key_ref, value_ref, low_ref, high_ref, out_ref,
                     max_ref, sum_ref, acc_ref):
    block = pl.program_id(0)
    heads = query_ref.shape[1] // HEAD_DIM
    first = span_ref[0] // KEY_BLOCK
    last = (span_ref[1] - 1) // KEY_BLOCK

    @pl.when(block == 0)
    def _():
        max_ref[...] = jnp.full(max_ref.shape, -1e30, jnp.float32)
        sum_ref[...] = jnp.zeros(sum_ref.shape, jnp.float32)
        acc_ref[...] = jnp.zeros(acc_ref.shape, jnp.float32)

    def step(masked):
        rows = query_ref.shape[0]
        if masked:
            key_index = block * KEY_BLOCK + lax.broadcasted_iota(jnp.int32, (rows, KEY_BLOCK), 1)
            valid = jnp.logical_and(key_index >= low_ref[...], key_index < high_ref[...])
        for head in range(heads):
            cols = slice(head * HEAD_DIM, (head + 1) * HEAD_DIM)
            raw = lax.dot_general(
                query_ref[:, cols], key_ref[:, cols], (((1,), (1,)), ((), ())),
                preferred_element_type=jnp.float32,
            )
            old_max = max_ref[head]
            if masked:
                block_max = jnp.max(jnp.where(valid, raw, -1e30), axis=1, keepdims=True)
            else:
                block_max = jnp.max(raw, axis=1, keepdims=True)
            new_max = jnp.maximum(old_max, block_max)
            probs = jnp.exp2((raw - new_max) * EXP2_SCALE)
            if masked:
                probs = jnp.where(valid, probs, 0.0)
            alpha = jnp.exp2((old_max - new_max) * EXP2_SCALE)
            sum_ref[head] = alpha * sum_ref[head] + jnp.sum(probs, axis=1, keepdims=True)
            acc_ref[:, cols] = alpha * acc_ref[:, cols] + jnp.dot(
                probs.astype(jnp.bfloat16), value_ref[:, cols],
                preferred_element_type=jnp.float32,
            )
            max_ref[head] = new_max

    touched = jnp.logical_and(block >= first, block <= last)
    whole_block = jnp.logical_and(
        block * KEY_BLOCK >= span_ref[2], (block + 1) * KEY_BLOCK <= span_ref[3]
    )

    @pl.when(jnp.logical_and(touched, whole_block))
    def _():
        step(False)

    @pl.when(jnp.logical_and(touched, jnp.logical_not(whole_block)))
    def _():
        step(True)

    @pl.when(block == pl.num_programs(0) - 1)
    def _():
        for head in range(heads):
            cols = slice(head * HEAD_DIM, (head + 1) * HEAD_DIM)
            out_ref[:, cols] = (acc_ref[:, cols] / sum_ref[head]).astype(out_ref.dtype)


def attention(span, query, packed, query_low, query_high):
    rows, width = query.shape
    blocks = packed.shape[0] // KEY_BLOCK

    def key_map(block, span_ref):
        first = span_ref[0] // KEY_BLOCK
        last = (span_ref[1] - 1) // KEY_BLOCK
        return (jnp.minimum(jnp.maximum(block, first), last), 0)

    def value_map(block, span_ref):
        first = span_ref[0] // KEY_BLOCK
        last = (span_ref[1] - 1) // KEY_BLOCK
        return (jnp.minimum(jnp.maximum(block, first), last), 1)

    whole = lambda block, span_ref: (0, 0)
    heads = width // HEAD_DIM
    return pl.pallas_call(
        attention_kernel,
        grid_spec=pltpu.PrefetchScalarGridSpec(
            num_scalar_prefetch=1,
            grid=(blocks,),
            in_specs=[
                pl.BlockSpec((rows, width), whole),
                pl.BlockSpec((KEY_BLOCK, width), key_map),
                pl.BlockSpec((KEY_BLOCK, width), value_map),
                pl.BlockSpec((rows, 1), whole),
                pl.BlockSpec((rows, 1), whole),
            ],
            out_specs=pl.BlockSpec((rows, width), whole),
            scratch_shapes=[
                pltpu.VMEM((heads, rows, 1), jnp.float32),
                pltpu.VMEM((heads, rows, 1), jnp.float32),
                pltpu.VMEM((rows, width), jnp.float32),
            ],
        ),
        out_shape=jax.ShapeDtypeStruct((rows, width), jnp.bfloat16),
    )(span, query, packed, packed, query_low, query_high)


def on_device(
    tokens, video_lengths, timestep, time_weight, block_mod, w_query, w_key, w_value, w_out
):
    tok_rows = tokens.shape[0]
    width = time_weight.shape[1] // 3
    full_rows = lax.all_gather(tokens, "tp", axis=1, tiled=True)
    time_value = timestep[0].astype(jnp.float32)
    sigma = noise_level(time_value)
    delta_sigma = noise_level(time_value - 1.0) - sigma
    half_freq = time_weight.shape[0] // 2
    frequency = jnp.exp(-math.log(10000.0) * jnp.arange(half_freq, dtype=jnp.float32) / half_freq)
    angle = 1000.0 * sigma * frequency
    embedding = jnp.concatenate([jnp.cos(angle), jnp.sin(angle)])
    modulation = jnp.sum(
        jax.nn.silu(embedding)[:, None] * time_weight, axis=0
    )
    modulation = modulation.reshape(3, width) + block_mod
    shift, scale, gate = (modulation[0], modulation[1], modulation[2])
    as_float = full_rows.astype(jnp.float32)
    mean = jnp.mean(as_float, axis=1, keepdims=True)
    centred = as_float - mean
    variance = jnp.mean(centred * centred, axis=1, keepdims=True)
    normed = (centred * lax.rsqrt(variance + 1e-06) * (1.0 + scale) + shift).astype(jnp.bfloat16)
    query = jnp.dot(normed, w_query, preferred_element_type=jnp.float32).astype(jnp.bfloat16)
    keys = jnp.dot(normed, w_key, preferred_element_type=jnp.float32).astype(jnp.bfloat16)
    values = jnp.dot(normed, w_value, preferred_element_type=jnp.float32).astype(jnp.bfloat16)
    start_row = lax.axis_index("req") * tok_rows
    query_index = start_row + jnp.arange(tok_rows, dtype=jnp.int32)
    video_ends = jnp.cumsum(video_lengths)
    video_starts = video_ends - video_lengths
    inside = jnp.logical_and(
        query_index[:, None] >= video_starts[None, :], query_index[:, None] < video_ends[None, :]
    )
    query_low = jnp.sum(jnp.where(inside, video_starts[None, :], 0), axis=1)
    query_high = jnp.sum(jnp.where(inside, video_ends[None, :], 0), axis=1)
    span = jnp.stack(
        [jnp.min(query_low), jnp.max(query_high), jnp.max(query_low), jnp.min(query_high)]
    ).astype(jnp.int32)
    packed = lax.all_gather(jnp.concatenate([keys, values], axis=1), "req", axis=0, tiled=True)
    attended = attention(span, query, packed, query_low[:, None], query_high[:, None])
    partial_value = jnp.dot(attended, w_out, preferred_element_type=jnp.float32)
    own_sum = lax.psum_scatter(
        partial_value.astype(jnp.bfloat16), "tp", scatter_dimension=1, tiled=True
    ).astype(jnp.float32)
    share = own_sum.shape[1]
    gate_share = lax.dynamic_slice_in_dim(gate, lax.axis_index("tp") * share, share)
    branch = gate_share[None, :] * own_sum
    velocity = branch.astype(jnp.bfloat16)
    stepped = (tokens.astype(jnp.float32) + delta_sigma * branch).astype(jnp.bfloat16)
    return (velocity, stepped)


def solution(mesh):
    return jax.shard_map(
        on_device,
        mesh=mesh,
        in_specs=(
            P("req", "tp"),
            P(),
            P(),
            P(),
            P(),
            P(None, "tp"),
            P(None, "tp"),
            P(None, "tp"),
            P("tp", None),
        ),
        out_specs=(P("req", "tp"), P("req", "tp")),
        check_vma=False,
    )
```

```python
import math

import jax
import jax.numpy as jnp
from jax import lax
from jax.experimental import pallas as pl
from jax.experimental.pallas import tpu as pltpu
from jax.sharding import PartitionSpec as P

HEAD_DIM = 128
STEPS = 1000
KEY_BLOCK = 1024
EXP2_SCALE = math.log2(math.e) / math.sqrt(HEAD_DIM)


def noise_level(step_value):
    frac = step_value / STEPS
    return 5.0 * frac / (1.0 + 4.0 * frac)


def attention_kernel(span_ref, query_ref, key_ref, value_ref, low_ref, high_ref, out_ref,
                     max_ref, sum_ref, acc_ref):
    block = pl.program_id(0)
    heads = query_ref.shape[1] // HEAD_DIM
    first = span_ref[0] // KEY_BLOCK
    last = (span_ref[1] - 1) // KEY_BLOCK

    @pl.when(block == 0)
    def _():
        max_ref[...] = jnp.full(max_ref.shape, -1e30, jnp.float32)
        sum_ref[...] = jnp.zeros(sum_ref.shape, jnp.float32)
        acc_ref[...] = jnp.zeros(acc_ref.shape, jnp.float32)

    def step(masked):
        rows = query_ref.shape[0]
        if masked:
            key_index = block * KEY_BLOCK + lax.broadcasted_iota(jnp.int32, (rows, KEY_BLOCK), 1)
            valid = jnp.logical_and(key_index >= low_ref[...], key_index < high_ref[...])
        for head in range(heads):
            cols = slice(head * HEAD_DIM, (head + 1) * HEAD_DIM)
            raw = lax.dot_general(
                query_ref[:, cols], key_ref[:, cols], (((1,), (1,)), ((), ())),
                preferred_element_type=jnp.float32,
            )
            old_max = max_ref[head]
            if masked:
                block_max = jnp.max(jnp.where(valid, raw, -1e30), axis=1, keepdims=True)
            else:
                block_max = jnp.max(raw, axis=1, keepdims=True)
            new_max = jnp.maximum(old_max, block_max)
            probs = jnp.exp2((raw - new_max) * EXP2_SCALE)
            if masked:
                probs = jnp.where(valid, probs, 0.0)
            alpha = jnp.exp2((old_max - new_max) * EXP2_SCALE)
            sum_ref[head] = alpha * sum_ref[head] + jnp.sum(probs, axis=1, keepdims=True)
            acc_ref[:, cols] = alpha * acc_ref[:, cols] + jnp.dot(
                probs.astype(jnp.bfloat16), value_ref[:, cols],
                preferred_element_type=jnp.float32,
            )
            max_ref[head] = new_max

    touched = jnp.logical_and(block >= first, block <= last)
    whole_block = jnp.logical_and(
        block * KEY_BLOCK >= span_ref[2], (block + 1) * KEY_BLOCK <= span_ref[3]
    )

    @pl.when(jnp.logical_and(touched, whole_block))
    def _():
        step(False)

    @pl.when(jnp.logical_and(touched, jnp.logical_not(whole_block)))
    def _():
        step(True)

    @pl.when(block == pl.num_programs(0) - 1)
    def _():
        for head in range(heads):
            cols = slice(head * HEAD_DIM, (head + 1) * HEAD_DIM)
            out_ref[:, cols] = (acc_ref[:, cols] / sum_ref[head]).astype(out_ref.dtype)


def attention(span, query, packed, query_low, query_high):
    rows, width = query.shape
    half_blocks = packed.shape[0] // KEY_BLOCK
    blocks = half_blocks * (packed.shape[1] // (2 * width))

    def clamp(block, span_ref):
        first = span_ref[0] // KEY_BLOCK
        last = (span_ref[1] - 1) // KEY_BLOCK
        return jnp.minimum(jnp.maximum(block, first), last)

    def key_map(block, span_ref):
        chosen = clamp(block, span_ref)
        return (chosen % half_blocks, 2 * (chosen // half_blocks))

    def value_map(block, span_ref):
        chosen = clamp(block, span_ref)
        return (chosen % half_blocks, 2 * (chosen // half_blocks) + 1)

    whole = lambda block, span_ref: (0, 0)
    heads = width // HEAD_DIM
    return pl.pallas_call(
        attention_kernel,
        grid_spec=pltpu.PrefetchScalarGridSpec(
            num_scalar_prefetch=1,
            grid=(blocks,),
            in_specs=[
                pl.BlockSpec((rows, width), whole),
                pl.BlockSpec((KEY_BLOCK, width), key_map),
                pl.BlockSpec((KEY_BLOCK, width), value_map),
                pl.BlockSpec((rows, 1), whole),
                pl.BlockSpec((rows, 1), whole),
            ],
            out_specs=pl.BlockSpec((rows, width), whole),
            scratch_shapes=[
                pltpu.VMEM((heads, rows, 1), jnp.float32),
                pltpu.VMEM((heads, rows, 1), jnp.float32),
                pltpu.VMEM((rows, width), jnp.float32),
            ],
        ),
        out_shape=jax.ShapeDtypeStruct((rows, width), jnp.bfloat16),
    )(span, query, packed, packed, query_low, query_high)


def on_device(
    tokens, video_lengths, timestep, time_weight, block_mod, w_query, w_key, w_value, w_out
):
    tok_rows = tokens.shape[0]
    width = time_weight.shape[1] // 3
    full_rows = lax.all_gather(tokens, "tp", axis=1, tiled=True)
    time_value = timestep[0].astype(jnp.float32)
    sigma = noise_level(time_value)
    delta_sigma = noise_level(time_value - 1.0) - sigma
    half_freq = time_weight.shape[0] // 2
    frequency = jnp.exp(-math.log(10000.0) * jnp.arange(half_freq, dtype=jnp.float32) / half_freq)
    angle = 1000.0 * sigma * frequency
    embedding = jnp.concatenate([jnp.cos(angle), jnp.sin(angle)])
    modulation = jnp.sum(
        jax.nn.silu(embedding)[:, None] * time_weight, axis=0
    )
    modulation = modulation.reshape(3, width) + block_mod
    shift, scale, gate = (modulation[0], modulation[1], modulation[2])
    as_float = full_rows.astype(jnp.float32)
    mean = jnp.mean(as_float, axis=1, keepdims=True)
    centred = as_float - mean
    variance = jnp.mean(centred * centred, axis=1, keepdims=True)
    normed = (centred * lax.rsqrt(variance + 1e-06) * (1.0 + scale) + shift).astype(jnp.bfloat16)
    query = jnp.dot(normed, w_query, preferred_element_type=jnp.float32).astype(jnp.bfloat16)
    keys = jnp.dot(normed, w_key, preferred_element_type=jnp.float32).astype(jnp.bfloat16)
    values = jnp.dot(normed, w_value, preferred_element_type=jnp.float32).astype(jnp.bfloat16)
    group_width = query.shape[1] // 2
    pair = lax.axis_index("pair")
    first_pair = pair == 0
    groups = []
    for group in range(2):
        cols = slice(group * group_width, (group + 1) * group_width)
        groups.append(jnp.concatenate([keys[:, cols], values[:, cols], query[:, cols]], axis=1))
    own_group = jnp.where(first_pair, groups[0], groups[1])
    sent_group = jnp.where(first_pair, groups[1], groups[0])
    received = lax.ppermute(sent_group, "pair", perm=[(0, 1), (1, 0)])
    halves = (jnp.where(first_pair, own_group, received), jnp.where(first_pair, received, own_group))
    packed_here = jnp.concatenate([half[:, : 2 * group_width] for half in halves], axis=1)
    packed = lax.all_gather(packed_here, "r", axis=0, tiled=True)
    video_ends = jnp.cumsum(video_lengths)
    video_starts = video_ends - video_lengths
    half_tokens = packed.shape[0]
    attended_halves = []
    for half_index, half in enumerate(halves):
        start_row = half_index * half_tokens + lax.axis_index("r") * tok_rows
        query_index = start_row + jnp.arange(tok_rows, dtype=jnp.int32)
        inside = jnp.logical_and(
            query_index[:, None] >= video_starts[None, :],
            query_index[:, None] < video_ends[None, :],
        )
        query_low = jnp.sum(jnp.where(inside, video_starts[None, :], 0), axis=1)
        query_high = jnp.sum(jnp.where(inside, video_ends[None, :], 0), axis=1)
        span = jnp.stack(
            [jnp.min(query_low), jnp.max(query_high), jnp.max(query_low), jnp.min(query_high)]
        ).astype(jnp.int32)
        attended_halves.append(
            attention(
                span, half[:, 2 * group_width :], packed, query_low[:, None], query_high[:, None]
            )
        )
    own_attended = jnp.where(first_pair, attended_halves[0], attended_halves[1])
    sent_attended = jnp.where(first_pair, attended_halves[1], attended_halves[0])
    other_attended = lax.ppermute(sent_attended, "pair", perm=[(0, 1), (1, 0)])
    attended = jnp.where(
        first_pair,
        jnp.concatenate([own_attended, other_attended], axis=1),
        jnp.concatenate([other_attended, own_attended], axis=1),
    )
    partial_value = jnp.dot(attended, w_out, preferred_element_type=jnp.float32)
    own_sum = lax.psum_scatter(
        partial_value.astype(jnp.bfloat16), "tp", scatter_dimension=1, tiled=True
    ).astype(jnp.float32)
    share = own_sum.shape[1]
    gate_share = lax.dynamic_slice_in_dim(gate, lax.axis_index("tp") * share, share)
    branch = gate_share[None, :] * own_sum
    velocity = branch.astype(jnp.bfloat16)
    stepped = (tokens.astype(jnp.float32) + delta_sigma * branch).astype(jnp.bfloat16)
    return (velocity, stepped)


def solution(mesh):
    req_size, tp_size = mesh.devices.shape
    split_mesh = jax.sharding.Mesh(
        mesh.devices.reshape(2, req_size // 2, tp_size), ("pair", "r", "tp")
    )
    rows = ("pair", "r")
    return jax.shard_map(
        on_device,
        mesh=split_mesh,
        in_specs=(
            P(rows, "tp"),
            P(),
            P(),
            P(),
            P(),
            P(None, "tp"),
            P(None, "tp"),
            P(None, "tp"),
            P("tp", None),
        ),
        out_specs=(P(rows, "tp"), P(rows, "tp")),
        check_vma=False,
    )
```

```python
import math

import jax
import jax.numpy as jnp
from jax import lax
from jax.experimental import pallas as pl
from jax.experimental.pallas import tpu as pltpu
from jax.sharding import PartitionSpec as P

HEAD_DIM = 128
STEPS = 1000
KEY_BLOCK = 2048
EXP2_SCALE = math.log2(math.e) / math.sqrt(HEAD_DIM)


def noise_level(step_value):
    frac = step_value / STEPS
    return 5.0 * frac / (1.0 + 4.0 * frac)


def attention_kernel(span_ref, query_ref, key_ref, value_ref, low_ref, high_ref, out_ref,
                     max_ref, sum_ref, acc_ref):
    block = pl.program_id(0)
    heads = query_ref.shape[1] // HEAD_DIM
    first = span_ref[0] // KEY_BLOCK
    last = (span_ref[1] - 1) // KEY_BLOCK

    @pl.when(block == 0)
    def _():
        max_ref[...] = jnp.full(max_ref.shape, -1e30, jnp.float32)
        sum_ref[...] = jnp.zeros(sum_ref.shape, jnp.float32)
        acc_ref[...] = jnp.zeros(acc_ref.shape, jnp.float32)

    def step(masked):
        rows = query_ref.shape[0]
        if masked:
            key_index = block * KEY_BLOCK + lax.broadcasted_iota(jnp.int32, (rows, KEY_BLOCK), 1)
            valid = jnp.logical_and(key_index >= low_ref[...], key_index < high_ref[...])
        for head in range(heads):
            cols = slice(head * HEAD_DIM, (head + 1) * HEAD_DIM)
            raw = lax.dot_general(
                query_ref[:, cols], key_ref[:, cols], (((1,), (1,)), ((), ())),
                preferred_element_type=jnp.float32,
            )
            old_max = max_ref[head]
            if masked:
                block_max = jnp.max(jnp.where(valid, raw, -1e30), axis=1, keepdims=True)
            else:
                block_max = jnp.max(raw, axis=1, keepdims=True)
            new_max = jnp.maximum(old_max, block_max)
            probs = jnp.exp2((raw - new_max) * EXP2_SCALE)
            if masked:
                probs = jnp.where(valid, probs, 0.0)
            alpha = jnp.exp2((old_max - new_max) * EXP2_SCALE)
            sum_ref[head] = alpha * sum_ref[head] + jnp.sum(probs, axis=1, keepdims=True)
            acc_ref[:, cols] = alpha * acc_ref[:, cols] + jnp.dot(
                probs.astype(jnp.bfloat16), value_ref[:, cols],
                preferred_element_type=jnp.float32,
            )
            max_ref[head] = new_max

    touched = jnp.logical_and(block >= first, block <= last)
    whole_block = jnp.logical_and(
        block * KEY_BLOCK >= span_ref[2], (block + 1) * KEY_BLOCK <= span_ref[3]
    )

    @pl.when(jnp.logical_and(touched, whole_block))
    def _():
        step(False)

    @pl.when(jnp.logical_and(touched, jnp.logical_not(whole_block)))
    def _():
        step(True)

    @pl.when(block == pl.num_programs(0) - 1)
    def _():
        for head in range(heads):
            cols = slice(head * HEAD_DIM, (head + 1) * HEAD_DIM)
            out_ref[:, cols] = (acc_ref[:, cols] / sum_ref[head]).astype(out_ref.dtype)


def attention(span, query, packed, query_low, query_high):
    rows, width = query.shape
    blocks = packed.shape[0] // KEY_BLOCK

    def key_map(block, span_ref):
        first = span_ref[0] // KEY_BLOCK
        last = (span_ref[1] - 1) // KEY_BLOCK
        return (jnp.minimum(jnp.maximum(block, first), last), 0)

    def value_map(block, span_ref):
        first = span_ref[0] // KEY_BLOCK
        last = (span_ref[1] - 1) // KEY_BLOCK
        return (jnp.minimum(jnp.maximum(block, first), last), 1)

    whole = lambda block, span_ref: (0, 0)
    heads = width // HEAD_DIM
    return pl.pallas_call(
        attention_kernel,
        grid_spec=pltpu.PrefetchScalarGridSpec(
            num_scalar_prefetch=1,
            grid=(blocks,),
            in_specs=[
                pl.BlockSpec((rows, width), whole),
                pl.BlockSpec((KEY_BLOCK, width), key_map),
                pl.BlockSpec((KEY_BLOCK, width), value_map),
                pl.BlockSpec((rows, 1), whole),
                pl.BlockSpec((rows, 1), whole),
            ],
            out_specs=pl.BlockSpec((rows, width), whole),
            scratch_shapes=[
                pltpu.VMEM((heads, rows, 1), jnp.float32),
                pltpu.VMEM((heads, rows, 1), jnp.float32),
                pltpu.VMEM((rows, width), jnp.float32),
            ],
        ),
        out_shape=jax.ShapeDtypeStruct((rows, width), jnp.bfloat16),
    )(span, query, packed, packed, query_low, query_high)


def on_device(
    tokens, video_lengths, timestep, time_weight, block_mod, w_query, w_key, w_value, w_out
):
    tok_rows = tokens.shape[0]
    width = time_weight.shape[1] // 3
    full_rows = lax.all_gather(tokens, "tp", axis=1, tiled=True)
    time_value = timestep[0].astype(jnp.float32)
    sigma = noise_level(time_value)
    delta_sigma = noise_level(time_value - 1.0) - sigma
    half_freq = time_weight.shape[0] // 2
    frequency = jnp.exp(-math.log(10000.0) * jnp.arange(half_freq, dtype=jnp.float32) / half_freq)
    angle = 1000.0 * sigma * frequency
    embedding = jnp.concatenate([jnp.cos(angle), jnp.sin(angle)])
    modulation = jnp.sum(
        jax.nn.silu(embedding)[:, None] * time_weight, axis=0
    )
    modulation = modulation.reshape(3, width) + block_mod
    shift, scale, gate = (modulation[0], modulation[1], modulation[2])
    as_float = full_rows.astype(jnp.float32)
    mean = jnp.mean(as_float, axis=1, keepdims=True)
    centred = as_float - mean
    variance = jnp.mean(centred * centred, axis=1, keepdims=True)
    normed = (centred * lax.rsqrt(variance + 1e-06) * (1.0 + scale) + shift).astype(jnp.bfloat16)
    query = jnp.dot(normed, w_query, preferred_element_type=jnp.float32).astype(jnp.bfloat16)
    keys = jnp.dot(normed, w_key, preferred_element_type=jnp.float32).astype(jnp.bfloat16)
    values = jnp.dot(normed, w_value, preferred_element_type=jnp.float32).astype(jnp.bfloat16)
    start_row = lax.axis_index("req") * tok_rows
    query_index = start_row + jnp.arange(tok_rows, dtype=jnp.int32)
    video_ends = jnp.cumsum(video_lengths)
    video_starts = video_ends - video_lengths
    inside = jnp.logical_and(
        query_index[:, None] >= video_starts[None, :], query_index[:, None] < video_ends[None, :]
    )
    query_low = jnp.sum(jnp.where(inside, video_starts[None, :], 0), axis=1)
    query_high = jnp.sum(jnp.where(inside, video_ends[None, :], 0), axis=1)
    span = jnp.stack(
        [jnp.min(query_low), jnp.max(query_high), jnp.max(query_low), jnp.min(query_high)]
    ).astype(jnp.int32)
    packed = lax.all_gather(jnp.concatenate([keys, values], axis=1), "req", axis=0, tiled=True)
    attended = attention(span, query, packed, query_low[:, None], query_high[:, None])
    partial_value = jnp.dot(attended, w_out, preferred_element_type=jnp.float32)
    own_sum = lax.psum_scatter(
        partial_value.astype(jnp.bfloat16), "tp", scatter_dimension=1, tiled=True
    ).astype(jnp.float32)
    share = own_sum.shape[1]
    gate_share = lax.dynamic_slice_in_dim(gate, lax.axis_index("tp") * share, share)
    branch = gate_share[None, :] * own_sum
    velocity = branch.astype(jnp.bfloat16)
    stepped = (tokens.astype(jnp.float32) + delta_sigma * branch).astype(jnp.bfloat16)
    return (velocity, stepped)


def solution(mesh):
    return jax.shard_map(
        on_device,
        mesh=mesh,
        in_specs=(
            P("req", "tp"),
            P(),
            P(),
            P(),
            P(),
            P(None, "tp"),
            P(None, "tp"),
            P(None, "tp"),
            P("tp", None),
        ),
        out_specs=(P("req", "tp"), P("req", "tp")),
        check_vma=False,
    )
```

```python
import math

import jax
import jax.numpy as jnp
from jax import lax
from jax.experimental import pallas as pl
from jax.experimental.pallas import tpu as pltpu
from jax.sharding import PartitionSpec as P

HEAD_DIM = 128
STEPS = 1000
KEY_BLOCK = 2048
EXP2_SCALE = math.log2(math.e) / math.sqrt(HEAD_DIM)


def noise_level(step_value):
    frac = step_value / STEPS
    return 5.0 * frac / (1.0 + 4.0 * frac)


def attention_kernel(span_ref, query_ref, key_ref, value_ref, low_ref, high_ref, out_ref,
                     max_ref, sum_ref, acc_ref):
    block = pl.program_id(0)
    heads = query_ref.shape[1] // HEAD_DIM
    first = span_ref[0] // KEY_BLOCK
    last = (span_ref[1] - 1) // KEY_BLOCK

    @pl.when(block == 0)
    def _():
        max_ref[...] = jnp.full(max_ref.shape, -1e30, jnp.float32)
        sum_ref[...] = jnp.zeros(sum_ref.shape, jnp.float32)
        acc_ref[...] = jnp.zeros(acc_ref.shape, jnp.float32)

    def step(masked):
        rows = query_ref.shape[0]
        if masked:
            key_index = block * KEY_BLOCK + lax.broadcasted_iota(jnp.int32, (rows, KEY_BLOCK), 1)
            valid = jnp.logical_and(key_index >= low_ref[...], key_index < high_ref[...])
        for head in range(heads):
            cols = slice(head * HEAD_DIM, (head + 1) * HEAD_DIM)
            raw = lax.dot_general(
                query_ref[:, cols], key_ref[:, cols], (((1,), (1,)), ((), ())),
                preferred_element_type=jnp.float32,
            )
            old_max = max_ref[head]
            if masked:
                block_max = jnp.max(jnp.where(valid, raw, -1e30), axis=1, keepdims=True)
            else:
                block_max = jnp.max(raw, axis=1, keepdims=True)
            new_max = jnp.maximum(old_max, block_max)
            probs = jnp.exp2((raw - new_max) * EXP2_SCALE)
            if masked:
                probs = jnp.where(valid, probs, 0.0)
            alpha = jnp.exp2((old_max - new_max) * EXP2_SCALE)
            sum_ref[head] = alpha * sum_ref[head] + jnp.sum(probs, axis=1, keepdims=True)
            acc_ref[:, cols] = alpha * acc_ref[:, cols] + jnp.dot(
                probs.astype(jnp.bfloat16), value_ref[:, cols],
                preferred_element_type=jnp.float32,
            )
            max_ref[head] = new_max

    touched = jnp.logical_and(block >= first, block <= last)
    whole_block = jnp.logical_and(
        block * KEY_BLOCK >= span_ref[2], (block + 1) * KEY_BLOCK <= span_ref[3]
    )

    @pl.when(jnp.logical_and(touched, whole_block))
    def _():
        step(False)

    @pl.when(jnp.logical_and(touched, jnp.logical_not(whole_block)))
    def _():
        step(True)

    @pl.when(block == pl.num_programs(0) - 1)
    def _():
        for head in range(heads):
            cols = slice(head * HEAD_DIM, (head + 1) * HEAD_DIM)
            out_ref[:, cols] = (acc_ref[:, cols] / sum_ref[head]).astype(out_ref.dtype)


def attention(span, query, packed, query_low, query_high):
    rows, width = query.shape
    blocks = packed.shape[0] // KEY_BLOCK

    def key_map(block, span_ref):
        first = span_ref[0] // KEY_BLOCK
        last = (span_ref[1] - 1) // KEY_BLOCK
        return (jnp.minimum(jnp.maximum(block, first), last), 0)

    def value_map(block, span_ref):
        first = span_ref[0] // KEY_BLOCK
        last = (span_ref[1] - 1) // KEY_BLOCK
        return (jnp.minimum(jnp.maximum(block, first), last), 1)

    whole = lambda block, span_ref: (0, 0)
    heads = width // HEAD_DIM
    return pl.pallas_call(
        attention_kernel,
        grid_spec=pltpu.PrefetchScalarGridSpec(
            num_scalar_prefetch=1,
            grid=(blocks,),
            in_specs=[
                pl.BlockSpec((rows, width), whole),
                pl.BlockSpec((KEY_BLOCK, width), key_map),
                pl.BlockSpec((KEY_BLOCK, width), value_map),
                pl.BlockSpec((rows, 1), whole),
                pl.BlockSpec((rows, 1), whole),
            ],
            out_specs=pl.BlockSpec((rows, width), whole),
            scratch_shapes=[
                pltpu.VMEM((heads, rows, 1), jnp.float32),
                pltpu.VMEM((heads, rows, 1), jnp.float32),
                pltpu.VMEM((rows, width), jnp.float32),
            ],
        ),
        out_shape=jax.ShapeDtypeStruct((rows, width), jnp.bfloat16),
    )(span, query, packed, packed, query_low, query_high)


def on_device(
    tokens, video_lengths, timestep, time_weight, block_mod, w_query, w_key, w_value, w_out
):
    tok_rows = tokens.shape[0]
    width = time_weight.shape[1] // 3
    full_rows = lax.all_gather(tokens, "tp", axis=1, tiled=True)
    time_value = timestep[0].astype(jnp.float32)
    sigma = noise_level(time_value)
    delta_sigma = noise_level(time_value - 1.0) - sigma
    half_freq = time_weight.shape[0] // 2
    frequency = jnp.exp(-math.log(10000.0) * jnp.arange(half_freq, dtype=jnp.float32) / half_freq)
    angle = 1000.0 * sigma * frequency
    embedding = jnp.concatenate([jnp.cos(angle), jnp.sin(angle)])
    modulation = jnp.sum(
        jax.nn.silu(embedding)[:, None] * time_weight, axis=0
    )
    modulation = modulation.reshape(3, width) + block_mod
    shift, scale, gate = (modulation[0], modulation[1], modulation[2])
    as_float = full_rows.astype(jnp.float32)
    mean = jnp.mean(as_float, axis=1, keepdims=True)
    centred = as_float - mean
    variance = jnp.mean(centred * centred, axis=1, keepdims=True)
    normed = (centred * lax.rsqrt(variance + 1e-06) * (1.0 + scale) + shift).astype(jnp.bfloat16)
    query = jnp.dot(normed, w_query, preferred_element_type=jnp.float32).astype(jnp.bfloat16)
    keys = jnp.dot(normed, w_key, preferred_element_type=jnp.float32).astype(jnp.bfloat16)
    values = jnp.dot(normed, w_value, preferred_element_type=jnp.float32).astype(jnp.bfloat16)
    start_row = lax.axis_index("req") * tok_rows
    query_index = start_row + jnp.arange(tok_rows, dtype=jnp.int32)
    video_ends = jnp.cumsum(video_lengths)
    video_starts = video_ends - video_lengths
    inside = jnp.logical_and(
        query_index[:, None] >= video_starts[None, :], query_index[:, None] < video_ends[None, :]
    )
    query_low = jnp.sum(jnp.where(inside, video_starts[None, :], 0), axis=1)
    query_high = jnp.sum(jnp.where(inside, video_ends[None, :], 0), axis=1)
    span = jnp.stack(
        [jnp.min(query_low), jnp.max(query_high), jnp.max(query_low), jnp.min(query_high)]
    ).astype(jnp.int32)
    packed = lax.all_gather(jnp.concatenate([keys, values], axis=1), "req", axis=0, tiled=True)
    attended = attention(span, query, packed, query_low[:, None], query_high[:, None])
    share = w_out.shape[1] // 2
    core = lax.axis_index("tp")
    swap = [(0, 1), (1, 0)]
    own_columns = lax.dynamic_slice_in_dim(w_out, core * share, share, axis=1)
    other_columns = lax.dynamic_slice_in_dim(w_out, (1 - core) * share, share, axis=1)
    partner_rows = lax.ppermute(other_columns, "tp", perm=swap)
    partner_attended = lax.ppermute(attended, "tp", perm=swap)
    projected = jnp.dot(attended, own_columns, preferred_element_type=jnp.float32) + jnp.dot(
        partner_attended, partner_rows, preferred_element_type=jnp.float32
    )
    gate_share = lax.dynamic_slice_in_dim(gate, core * share, share)
    branch = gate_share[None, :] * projected
    velocity = branch.astype(jnp.bfloat16)
    stepped = (tokens.astype(jnp.float32) + delta_sigma * branch).astype(jnp.bfloat16)
    return (velocity, stepped)


def solution(mesh):
    return jax.shard_map(
        on_device,
        mesh=mesh,
        in_specs=(
            P("req", "tp"),
            P(),
            P(),
            P(),
            P(),
            P(None, "tp"),
            P(None, "tp"),
            P(None, "tp"),
            P("tp", None),
        ),
        out_specs=(P("req", "tp"), P("req", "tp")),
        check_vma=False,
    )
```

```python
import math

import jax
import jax.numpy as jnp
from jax import lax
from jax.experimental import pallas as pl
from jax.experimental.pallas import tpu as pltpu
from jax.sharding import PartitionSpec as P

HEAD_DIM = 128
STEPS = 1000
KEY_BLOCK = 2048
EXP2_SCALE = math.log2(math.e) / math.sqrt(HEAD_DIM)


def noise_level(step_value):
    frac = step_value / STEPS
    return 5.0 * frac / (1.0 + 4.0 * frac)


def attention_kernel(span_ref, query_ref, key_ref, value_ref, low_ref, high_ref, out_ref,
                     max_ref, sum_ref, acc_ref):
    block = pl.program_id(0)
    heads = query_ref.shape[1] // HEAD_DIM
    first = span_ref[0] // KEY_BLOCK
    last = (span_ref[1] - 1) // KEY_BLOCK

    @pl.when(block == 0)
    def _():
        max_ref[...] = jnp.full(max_ref.shape, -1e30, jnp.float32)
        sum_ref[...] = jnp.zeros(sum_ref.shape, jnp.float32)
        acc_ref[...] = jnp.zeros(acc_ref.shape, jnp.float32)

    def step(masked):
        rows = query_ref.shape[0]
        if masked:
            key_index = block * KEY_BLOCK + lax.broadcasted_iota(jnp.int32, (rows, KEY_BLOCK), 1)
            valid = jnp.logical_and(key_index >= low_ref[...], key_index < high_ref[...])
        for head in range(heads):
            cols = slice(head * HEAD_DIM, (head + 1) * HEAD_DIM)
            raw = lax.dot_general(
                query_ref[:, cols], key_ref[:, cols], (((1,), (1,)), ((), ())),
                preferred_element_type=jnp.float32,
            )
            old_max = max_ref[head]
            if masked:
                block_max = jnp.max(jnp.where(valid, raw, -1e30), axis=1, keepdims=True)
            else:
                block_max = jnp.max(raw, axis=1, keepdims=True)
            new_max = jnp.maximum(old_max, block_max)
            probs = jnp.exp2((raw - new_max) * EXP2_SCALE)
            if masked:
                probs = jnp.where(valid, probs, 0.0)
            alpha = jnp.exp2((old_max - new_max) * EXP2_SCALE)
            sum_ref[head] = alpha * sum_ref[head] + jnp.sum(probs, axis=1, keepdims=True)
            acc_ref[:, cols] = alpha * acc_ref[:, cols] + jnp.dot(
                probs.astype(jnp.bfloat16), value_ref[:, cols],
                preferred_element_type=jnp.float32,
            )
            max_ref[head] = new_max

    touched = jnp.logical_and(block >= first, block <= last)
    whole_block = jnp.logical_and(
        block * KEY_BLOCK >= span_ref[2], (block + 1) * KEY_BLOCK <= span_ref[3]
    )

    @pl.when(jnp.logical_and(touched, whole_block))
    def _():
        step(False)

    @pl.when(jnp.logical_and(touched, jnp.logical_not(whole_block)))
    def _():
        step(True)

    @pl.when(block == pl.num_programs(0) - 1)
    def _():
        for head in range(heads):
            cols = slice(head * HEAD_DIM, (head + 1) * HEAD_DIM)
            out_ref[:, cols] = (acc_ref[:, cols] / sum_ref[head]).astype(out_ref.dtype)


def attention(span, query, packed, query_low, query_high):
    rows, width = query.shape
    blocks = packed.shape[0] // KEY_BLOCK

    def key_map(block, span_ref):
        first = span_ref[0] // KEY_BLOCK
        last = (span_ref[1] - 1) // KEY_BLOCK
        return (jnp.minimum(jnp.maximum(block, first), last), 0)

    def value_map(block, span_ref):
        first = span_ref[0] // KEY_BLOCK
        last = (span_ref[1] - 1) // KEY_BLOCK
        return (jnp.minimum(jnp.maximum(block, first), last), 1)

    whole = lambda block, span_ref: (0, 0)
    heads = width // HEAD_DIM
    return pl.pallas_call(
        attention_kernel,
        grid_spec=pltpu.PrefetchScalarGridSpec(
            num_scalar_prefetch=1,
            grid=(blocks,),
            in_specs=[
                pl.BlockSpec((rows, width), whole),
                pl.BlockSpec((KEY_BLOCK, width), key_map),
                pl.BlockSpec((KEY_BLOCK, width), value_map),
                pl.BlockSpec((rows, 1), whole),
                pl.BlockSpec((rows, 1), whole),
            ],
            out_specs=pl.BlockSpec((rows, width), whole),
            scratch_shapes=[
                pltpu.VMEM((heads, rows, 1), jnp.float32),
                pltpu.VMEM((heads, rows, 1), jnp.float32),
                pltpu.VMEM((rows, width), jnp.float32),
            ],
        ),
        out_shape=jax.ShapeDtypeStruct((rows, width), jnp.bfloat16),
    )(span, query, packed, packed, query_low, query_high)


def on_device(
    tokens, video_lengths, timestep, time_weight, block_mod, w_query, w_key, w_value, w_out
):
    tok_rows = tokens.shape[0]
    width = time_weight.shape[1] // 3
    first_core = lax.axis_index("tp") == 0
    other_half = lax.ppermute(tokens, "tp", perm=[(0, 1), (1, 0)])
    full_rows = jnp.where(
        first_core,
        jnp.concatenate([tokens, other_half], axis=1),
        jnp.concatenate([other_half, tokens], axis=1),
    )
    time_value = timestep[0].astype(jnp.float32)
    sigma = noise_level(time_value)
    delta_sigma = noise_level(time_value - 1.0) - sigma
    half_freq = time_weight.shape[0] // 2
    frequency = jnp.exp(-math.log(10000.0) * jnp.arange(half_freq, dtype=jnp.float32) / half_freq)
    angle = 1000.0 * sigma * frequency
    embedding = jnp.concatenate([jnp.cos(angle), jnp.sin(angle)])
    activated = jax.nn.silu(embedding)[:, None]
    shift_scale = jnp.sum(activated * time_weight[:, : 2 * width], axis=0).reshape(2, width)
    shift = shift_scale[0] + block_mod[0]
    scale = shift_scale[1] + block_mod[1]
    gate = jnp.sum(activated * time_weight[:, 2 * width :], axis=0) + block_mod[2]
    as_float = full_rows.astype(jnp.float32)
    mean = jnp.mean(as_float, axis=1, keepdims=True)
    centred = as_float - mean
    variance = jnp.mean(centred * centred, axis=1, keepdims=True)
    normed = (centred * lax.rsqrt(variance + 1e-06) * (1.0 + scale) + shift).astype(jnp.bfloat16)
    query = jnp.dot(normed, w_query, preferred_element_type=jnp.float32).astype(jnp.bfloat16)
    keys = jnp.dot(normed, w_key, preferred_element_type=jnp.float32).astype(jnp.bfloat16)
    values = jnp.dot(normed, w_value, preferred_element_type=jnp.float32).astype(jnp.bfloat16)
    start_row = lax.axis_index("req") * tok_rows
    query_index = start_row + jnp.arange(tok_rows, dtype=jnp.int32)
    video_ends = jnp.cumsum(video_lengths)
    video_starts = video_ends - video_lengths
    inside = jnp.logical_and(
        query_index[:, None] >= video_starts[None, :], query_index[:, None] < video_ends[None, :]
    )
    query_low = jnp.sum(jnp.where(inside, video_starts[None, :], 0), axis=1)
    query_high = jnp.sum(jnp.where(inside, video_ends[None, :], 0), axis=1)
    span = jnp.stack(
        [jnp.min(query_low), jnp.max(query_high), jnp.max(query_low), jnp.min(query_high)]
    ).astype(jnp.int32)
    packed = lax.all_gather(jnp.concatenate([keys, values], axis=1), "req", axis=0, tiled=True)
    attended = attention(span, query, packed, query_low[:, None], query_high[:, None])
    share = w_out.shape[1] // 2
    core = lax.axis_index("tp")
    swap = [(0, 1), (1, 0)]
    own_columns = lax.dynamic_slice_in_dim(w_out, core * share, share, axis=1)
    other_columns = lax.dynamic_slice_in_dim(w_out, (1 - core) * share, share, axis=1)
    partner_rows = lax.ppermute(other_columns, "tp", perm=swap)
    partner_attended = lax.ppermute(attended, "tp", perm=swap)
    projected = jnp.dot(attended, own_columns, preferred_element_type=jnp.float32) + jnp.dot(
        partner_attended, partner_rows, preferred_element_type=jnp.float32
    )
    gate_share = lax.dynamic_slice_in_dim(gate, core * share, share)
    branch = gate_share[None, :] * projected
    velocity = branch.astype(jnp.bfloat16)
    stepped = (tokens.astype(jnp.float32) + delta_sigma * branch).astype(jnp.bfloat16)
    return (velocity, stepped)


def solution(mesh):
    return jax.shard_map(
        on_device,
        mesh=mesh,
        in_specs=(
            P("req", "tp"),
            P(),
            P(),
            P(),
            P(),
            P(None, "tp"),
            P(None, "tp"),
            P(None, "tp"),
            P("tp", None),
        ),
        out_specs=(P("req", "tp"), P("req", "tp")),
        check_vma=False,
    )
```

```python
import math

import jax
import jax.numpy as jnp
from jax import lax
from jax.experimental import pallas as pl
from jax.experimental.pallas import tpu as pltpu
from jax.sharding import PartitionSpec as P

HEAD_DIM = 128
STEPS = 1000
KEY_BLOCK = 2048
EXP2_SCALE = math.log2(math.e) / math.sqrt(HEAD_DIM)


def noise_level(step_value):
    frac = step_value / STEPS
    return 5.0 * frac / (1.0 + 4.0 * frac)


def attention_kernel(span_ref, query_ref, key_ref, value_ref, low_ref, high_ref, out_ref,
                     max_ref, sum_ref, acc_ref):
    block = pl.program_id(0)
    heads = query_ref.shape[1] // HEAD_DIM
    first = span_ref[0] // KEY_BLOCK
    last = (span_ref[1] - 1) // KEY_BLOCK

    @pl.when(block == 0)
    def _():
        max_ref[...] = jnp.full(max_ref.shape, -1e30, jnp.float32)
        sum_ref[...] = jnp.zeros(sum_ref.shape, jnp.float32)
        acc_ref[...] = jnp.zeros(acc_ref.shape, jnp.float32)

    def step(masked, offset, size):
        rows = query_ref.shape[0]
        keys = pl.ds(offset, size)
        if masked:
            key_index = (
                block * KEY_BLOCK + offset + lax.broadcasted_iota(jnp.int32, (rows, size), 1)
            )
            valid = jnp.logical_and(key_index >= low_ref[...], key_index < high_ref[...])
        for head in range(heads):
            cols = slice(head * HEAD_DIM, (head + 1) * HEAD_DIM)
            raw = lax.dot_general(
                query_ref[:, cols], key_ref[keys, cols], (((1,), (1,)), ((), ())),
                preferred_element_type=jnp.float32,
            )
            old_max = max_ref[head]
            if masked:
                block_max = jnp.max(jnp.where(valid, raw, -1e30), axis=1, keepdims=True)
            else:
                block_max = jnp.max(raw, axis=1, keepdims=True)
            new_max = jnp.maximum(old_max, block_max)
            probs = jnp.exp2((raw - new_max) * EXP2_SCALE)
            if masked:
                probs = jnp.where(valid, probs, 0.0)
            alpha = jnp.exp2((old_max - new_max) * EXP2_SCALE)
            sum_ref[head] = alpha * sum_ref[head] + jnp.sum(probs, axis=1, keepdims=True)
            acc_ref[:, cols] = alpha * acc_ref[:, cols] + jnp.dot(
                probs.astype(jnp.bfloat16), value_ref[keys, cols],
                preferred_element_type=jnp.float32,
            )
            max_ref[head] = new_max

    half = KEY_BLOCK // 2
    base = block * KEY_BLOCK
    touched = jnp.logical_and(block >= first, block <= last)
    whole_block = jnp.logical_and(base >= span_ref[2], base + KEY_BLOCK <= span_ref[3])
    edge = jnp.logical_and(touched, jnp.logical_not(whole_block))
    need_low = jnp.logical_and(base < span_ref[1], base + half > span_ref[0])
    need_high = jnp.logical_and(base + half < span_ref[1], base + KEY_BLOCK > span_ref[0])

    @pl.when(jnp.logical_and(touched, whole_block))
    def _():
        step(False, 0, KEY_BLOCK)

    @pl.when(jnp.logical_and(edge, jnp.logical_and(need_low, need_high)))
    def _():
        step(True, 0, KEY_BLOCK)

    @pl.when(jnp.logical_and(edge, jnp.logical_and(need_low, jnp.logical_not(need_high))))
    def _():
        step(True, 0, half)

    @pl.when(jnp.logical_and(edge, jnp.logical_and(need_high, jnp.logical_not(need_low))))
    def _():
        step(True, half, half)

    @pl.when(block == pl.num_programs(0) - 1)
    def _():
        for head in range(heads):
            cols = slice(head * HEAD_DIM, (head + 1) * HEAD_DIM)
            out_ref[:, cols] = (acc_ref[:, cols] / sum_ref[head]).astype(out_ref.dtype)


def attention(span, query, packed, query_low, query_high):
    rows, width = query.shape
    blocks = packed.shape[0] // KEY_BLOCK

    def key_map(block, span_ref):
        first = span_ref[0] // KEY_BLOCK
        last = (span_ref[1] - 1) // KEY_BLOCK
        return (jnp.minimum(jnp.maximum(block, first), last), 0)

    def value_map(block, span_ref):
        first = span_ref[0] // KEY_BLOCK
        last = (span_ref[1] - 1) // KEY_BLOCK
        return (jnp.minimum(jnp.maximum(block, first), last), 1)

    whole = lambda block, span_ref: (0, 0)
    heads = width // HEAD_DIM
    return pl.pallas_call(
        attention_kernel,
        grid_spec=pltpu.PrefetchScalarGridSpec(
            num_scalar_prefetch=1,
            grid=(blocks,),
            in_specs=[
                pl.BlockSpec((rows, width), whole),
                pl.BlockSpec((KEY_BLOCK, width), key_map),
                pl.BlockSpec((KEY_BLOCK, width), value_map),
                pl.BlockSpec((rows, 1), whole),
                pl.BlockSpec((rows, 1), whole),
            ],
            out_specs=pl.BlockSpec((rows, width), whole),
            scratch_shapes=[
                pltpu.VMEM((heads, rows, 1), jnp.float32),
                pltpu.VMEM((heads, rows, 1), jnp.float32),
                pltpu.VMEM((rows, width), jnp.float32),
            ],
        ),
        out_shape=jax.ShapeDtypeStruct((rows, width), jnp.bfloat16),
    )(span, query, packed, packed, query_low, query_high)


def on_device(
    tokens, video_lengths, timestep, time_weight, block_mod, w_query, w_key, w_value, w_out
):
    tok_rows = tokens.shape[0]
    width = time_weight.shape[1] // 3
    first_core = lax.axis_index("tp") == 0
    other_half = lax.ppermute(tokens, "tp", perm=[(0, 1), (1, 0)])
    full_rows = jnp.where(
        first_core,
        jnp.concatenate([tokens, other_half], axis=1),
        jnp.concatenate([other_half, tokens], axis=1),
    )
    time_value = timestep[0].astype(jnp.float32)
    sigma = noise_level(time_value)
    delta_sigma = noise_level(time_value - 1.0) - sigma
    half_freq = time_weight.shape[0] // 2
    frequency = jnp.exp(-math.log(10000.0) * jnp.arange(half_freq, dtype=jnp.float32) / half_freq)
    angle = 1000.0 * sigma * frequency
    embedding = jnp.concatenate([jnp.cos(angle), jnp.sin(angle)])
    activated = jax.nn.silu(embedding)[:, None]
    shift_scale = jnp.sum(activated * time_weight[:, : 2 * width], axis=0).reshape(2, width)
    shift = shift_scale[0] + block_mod[0]
    scale = shift_scale[1] + block_mod[1]
    gate = jnp.sum(activated * time_weight[:, 2 * width :], axis=0) + block_mod[2]
    as_float = full_rows.astype(jnp.float32)
    mean = jnp.mean(as_float, axis=1, keepdims=True)
    centred = as_float - mean
    variance = jnp.mean(centred * centred, axis=1, keepdims=True)
    normed = (centred * lax.rsqrt(variance + 1e-06) * (1.0 + scale) + shift).astype(jnp.bfloat16)
    query = jnp.dot(normed, w_query, preferred_element_type=jnp.float32).astype(jnp.bfloat16)
    keys = jnp.dot(normed, w_key, preferred_element_type=jnp.float32).astype(jnp.bfloat16)
    values = jnp.dot(normed, w_value, preferred_element_type=jnp.float32).astype(jnp.bfloat16)
    start_row = lax.axis_index("req") * tok_rows
    query_index = start_row + jnp.arange(tok_rows, dtype=jnp.int32)
    video_ends = jnp.cumsum(video_lengths)
    video_starts = video_ends - video_lengths
    inside = jnp.logical_and(
        query_index[:, None] >= video_starts[None, :], query_index[:, None] < video_ends[None, :]
    )
    query_low = jnp.sum(jnp.where(inside, video_starts[None, :], 0), axis=1)
    query_high = jnp.sum(jnp.where(inside, video_ends[None, :], 0), axis=1)
    span = jnp.stack(
        [jnp.min(query_low), jnp.max(query_high), jnp.max(query_low), jnp.min(query_high)]
    ).astype(jnp.int32)
    packed = lax.all_gather(jnp.concatenate([keys, values], axis=1), "req", axis=0, tiled=True)
    attended = attention(span, query, packed, query_low[:, None], query_high[:, None])
    share = w_out.shape[1] // 2
    core = lax.axis_index("tp")
    swap = [(0, 1), (1, 0)]
    own_columns = lax.dynamic_slice_in_dim(w_out, core * share, share, axis=1)
    other_columns = lax.dynamic_slice_in_dim(w_out, (1 - core) * share, share, axis=1)
    partner_rows = lax.ppermute(other_columns, "tp", perm=swap)
    partner_attended = lax.ppermute(attended, "tp", perm=swap)
    projected = jnp.dot(attended, own_columns, preferred_element_type=jnp.float32) + jnp.dot(
        partner_attended, partner_rows, preferred_element_type=jnp.float32
    )
    gate_share = lax.dynamic_slice_in_dim(gate, core * share, share)
    branch = gate_share[None, :] * projected
    velocity = branch.astype(jnp.bfloat16)
    stepped = (tokens.astype(jnp.float32) + delta_sigma * branch).astype(jnp.bfloat16)
    return (velocity, stepped)


def solution(mesh):
    return jax.shard_map(
        on_device,
        mesh=mesh,
        in_specs=(
            P("req", "tp"),
            P(),
            P(),
            P(),
            P(),
            P(None, "tp"),
            P(None, "tp"),
            P(None, "tp"),
            P("tp", None),
        ),
        out_specs=(P("req", "tp"), P("req", "tp")),
        check_vma=False,
    )
```

```python
import math

import jax
import jax.numpy as jnp
from jax import lax
from jax.experimental import pallas as pl
from jax.experimental.pallas import tpu as pltpu
from jax.sharding import PartitionSpec as P

HEAD_DIM = 128
STEPS = 1000
KEY_BLOCK = 2048
EXP2_SCALE = math.log2(math.e) / math.sqrt(HEAD_DIM)


def noise_level(step_value):
    frac = step_value / STEPS
    return 5.0 * frac / (1.0 + 4.0 * frac)


def attention_kernel(span_ref, query_ref, key_ref, value_ref, low_ref, high_ref, out_ref,
                     max_ref, sum_ref, acc_ref):
    block = pl.program_id(0)
    heads = query_ref.shape[1] // HEAD_DIM
    first = span_ref[0] // KEY_BLOCK
    last = (span_ref[1] - 1) // KEY_BLOCK

    @pl.when(block == 0)
    def _():
        max_ref[...] = jnp.full(max_ref.shape, -1e30, jnp.float32)
        sum_ref[...] = jnp.zeros(sum_ref.shape, jnp.float32)
        acc_ref[...] = jnp.zeros(acc_ref.shape, jnp.float32)

    def step(masked):
        rows = query_ref.shape[0]
        if masked:
            key_index = block * KEY_BLOCK + lax.broadcasted_iota(jnp.int32, (rows, KEY_BLOCK), 1)
            valid = jnp.logical_and(key_index >= low_ref[...], key_index < high_ref[...])
        for head in range(heads):
            cols = slice(head * HEAD_DIM, (head + 1) * HEAD_DIM)
            raw = lax.dot_general(
                query_ref[:, cols], key_ref[:, cols], (((1,), (1,)), ((), ())),
                preferred_element_type=jnp.float32,
            )
            old_max = max_ref[head]
            if masked:
                block_max = jnp.max(jnp.where(valid, raw, -1e30), axis=1, keepdims=True)
            else:
                block_max = jnp.max(raw, axis=1, keepdims=True)
            new_max = jnp.maximum(old_max, block_max)
            probs = jnp.exp2((raw - new_max) * EXP2_SCALE)
            if masked:
                probs = jnp.where(valid, probs, 0.0)
            alpha = jnp.exp2((old_max - new_max) * EXP2_SCALE)
            sum_ref[head] = alpha * sum_ref[head] + jnp.sum(probs, axis=1, keepdims=True)
            acc_ref[:, cols] = alpha * acc_ref[:, cols] + jnp.dot(
                probs.astype(jnp.bfloat16), value_ref[:, cols],
                preferred_element_type=jnp.float32,
            )
            max_ref[head] = new_max

    touched = jnp.logical_and(block >= first, block <= last)
    whole_block = jnp.logical_and(
        block * KEY_BLOCK >= span_ref[2], (block + 1) * KEY_BLOCK <= span_ref[3]
    )

    @pl.when(jnp.logical_and(touched, whole_block))
    def _():
        step(False)

    @pl.when(jnp.logical_and(touched, jnp.logical_not(whole_block)))
    def _():
        step(True)

    @pl.when(block == pl.num_programs(0) - 1)
    def _():
        for head in range(heads):
            cols = slice(head * HEAD_DIM, (head + 1) * HEAD_DIM)
            out_ref[:, cols] = (acc_ref[:, cols] / sum_ref[head]).astype(out_ref.dtype)


def attention(span, query, packed, query_low, query_high):
    rows, width = query.shape
    blocks = packed.shape[0] // KEY_BLOCK

    def key_map(block, span_ref):
        first = span_ref[0] // KEY_BLOCK
        last = (span_ref[1] - 1) // KEY_BLOCK
        return (jnp.minimum(jnp.maximum(block, first), last), 0)

    def value_map(block, span_ref):
        first = span_ref[0] // KEY_BLOCK
        last = (span_ref[1] - 1) // KEY_BLOCK
        return (jnp.minimum(jnp.maximum(block, first), last), 1)

    whole = lambda block, span_ref: (0, 0)
    heads = width // HEAD_DIM
    return pl.pallas_call(
        attention_kernel,
        grid_spec=pltpu.PrefetchScalarGridSpec(
            num_scalar_prefetch=1,
            grid=(blocks,),
            in_specs=[
                pl.BlockSpec((rows, width), whole),
                pl.BlockSpec((KEY_BLOCK, width), key_map),
                pl.BlockSpec((KEY_BLOCK, width), value_map),
                pl.BlockSpec((rows, 1), whole),
                pl.BlockSpec((rows, 1), whole),
            ],
            out_specs=pl.BlockSpec((rows, width), whole),
            scratch_shapes=[
                pltpu.VMEM((heads, rows, 1), jnp.float32),
                pltpu.VMEM((heads, rows, 1), jnp.float32),
                pltpu.VMEM((rows, width), jnp.float32),
            ],
        ),
        out_shape=jax.ShapeDtypeStruct((rows, width), jnp.bfloat16),
    )(span, query, packed, packed, query_low, query_high)


def project_kernel(rows_ref, shift_ref, scale_ref, key_w_ref, value_w_ref, packed_ref, normed_ref):
    as_float = rows_ref[...].astype(jnp.float32)
    mean = jnp.mean(as_float, axis=1, keepdims=True)
    centred = as_float - mean
    variance = jnp.mean(centred * centred, axis=1, keepdims=True)
    normed = (
        centred * lax.rsqrt(variance + 1e-06) * (1.0 + scale_ref[...]) + shift_ref[...]
    ).astype(jnp.bfloat16)
    normed_ref[...] = normed
    width = key_w_ref.shape[1]
    packed_ref[:, :width] = jnp.dot(
        normed, key_w_ref[...], preferred_element_type=jnp.float32
    ).astype(jnp.bfloat16)
    packed_ref[:, width:] = jnp.dot(
        normed, value_w_ref[...], preferred_element_type=jnp.float32
    ).astype(jnp.bfloat16)


def project(full_rows, shift, scale, w_key, w_value):
    rows, features = full_rows.shape
    return pl.pallas_call(
        project_kernel,
        out_shape=(
            jax.ShapeDtypeStruct((rows, 2 * w_key.shape[1]), jnp.bfloat16),
            jax.ShapeDtypeStruct((rows, features), jnp.bfloat16),
        ),
    )(full_rows, shift[None, :], scale[None, :], w_key, w_value)


def on_device(
    tokens, video_lengths, timestep, time_weight, block_mod, w_query, w_key, w_value, w_out
):
    tok_rows = tokens.shape[0]
    width = time_weight.shape[1] // 3
    first_core = lax.axis_index("tp") == 0
    other_half = lax.ppermute(tokens, "tp", perm=[(0, 1), (1, 0)])
    full_rows = jnp.where(
        first_core,
        jnp.concatenate([tokens, other_half], axis=1),
        jnp.concatenate([other_half, tokens], axis=1),
    )
    time_value = timestep[0].astype(jnp.float32)
    sigma = noise_level(time_value)
    delta_sigma = noise_level(time_value - 1.0) - sigma
    half_freq = time_weight.shape[0] // 2
    frequency = jnp.exp(-math.log(10000.0) * jnp.arange(half_freq, dtype=jnp.float32) / half_freq)
    angle = 1000.0 * sigma * frequency
    embedding = jnp.concatenate([jnp.cos(angle), jnp.sin(angle)])
    activated = jax.nn.silu(embedding)[:, None]
    shift_scale = jnp.sum(activated * time_weight[:, : 2 * width], axis=0).reshape(2, width)
    shift = shift_scale[0] + block_mod[0]
    scale = shift_scale[1] + block_mod[1]
    gate = jnp.sum(activated * time_weight[:, 2 * width :], axis=0) + block_mod[2]
    kv_rows, normed = project(full_rows, shift, scale, w_key, w_value)
    query = jnp.dot(normed, w_query, preferred_element_type=jnp.float32).astype(jnp.bfloat16)
    start_row = lax.axis_index("req") * tok_rows
    query_index = start_row + jnp.arange(tok_rows, dtype=jnp.int32)
    video_ends = jnp.cumsum(video_lengths)
    video_starts = video_ends - video_lengths
    inside = jnp.logical_and(
        query_index[:, None] >= video_starts[None, :], query_index[:, None] < video_ends[None, :]
    )
    query_low = jnp.sum(jnp.where(inside, video_starts[None, :], 0), axis=1)
    query_high = jnp.sum(jnp.where(inside, video_ends[None, :], 0), axis=1)
    span = jnp.stack(
        [jnp.min(query_low), jnp.max(query_high), jnp.max(query_low), jnp.min(query_high)]
    ).astype(jnp.int32)
    packed = lax.all_gather(kv_rows, "req", axis=0, tiled=True)
    attended = attention(span, query, packed, query_low[:, None], query_high[:, None])
    share = w_out.shape[1] // 2
    core = lax.axis_index("tp")
    swap = [(0, 1), (1, 0)]
    own_columns = lax.dynamic_slice_in_dim(w_out, core * share, share, axis=1)
    other_columns = lax.dynamic_slice_in_dim(w_out, (1 - core) * share, share, axis=1)
    partner_rows = lax.ppermute(other_columns, "tp", perm=swap)
    partner_attended = lax.ppermute(attended, "tp", perm=swap)
    projected = jnp.dot(attended, own_columns, preferred_element_type=jnp.float32) + jnp.dot(
        partner_attended, partner_rows, preferred_element_type=jnp.float32
    )
    gate_share = lax.dynamic_slice_in_dim(gate, core * share, share)
    branch = gate_share[None, :] * projected
    velocity = branch.astype(jnp.bfloat16)
    stepped = (tokens.astype(jnp.float32) + delta_sigma * branch).astype(jnp.bfloat16)
    return (velocity, stepped)


def solution(mesh):
    return jax.shard_map(
        on_device,
        mesh=mesh,
        in_specs=(
            P("req", "tp"),
            P(),
            P(),
            P(),
            P(),
            P(None, "tp"),
            P(None, "tp"),
            P(None, "tp"),
            P("tp", None),
        ),
        out_specs=(P("req", "tp"), P("req", "tp")),
        check_vma=False,
    )
```

```python
import math

import jax
import jax.numpy as jnp
from jax import lax
from jax.experimental import pallas as pl
from jax.experimental.pallas import tpu as pltpu
from jax.sharding import PartitionSpec as P

HEAD_DIM = 128
STEPS = 1000
KEY_BLOCK = 2048
EXP2_SCALE = math.log2(math.e) / math.sqrt(HEAD_DIM)


def noise_level(step_value):
    frac = step_value / STEPS
    return 5.0 * frac / (1.0 + 4.0 * frac)


def attention_kernel(span_ref, query_ref, key_ref, value_ref, low_ref, high_ref, own_w_ref,
                     other_w_ref, own_ref, other_ref, max_ref, sum_ref, acc_ref, attended_ref):
    block = pl.program_id(0)
    heads = query_ref.shape[1] // HEAD_DIM
    first = span_ref[0] // KEY_BLOCK
    last = (span_ref[1] - 1) // KEY_BLOCK

    @pl.when(block == 0)
    def _():
        max_ref[...] = jnp.full(max_ref.shape, -1e30, jnp.float32)
        sum_ref[...] = jnp.zeros(sum_ref.shape, jnp.float32)
        acc_ref[...] = jnp.zeros(acc_ref.shape, jnp.float32)

    def step(masked):
        rows = query_ref.shape[0]
        if masked:
            key_index = block * KEY_BLOCK + lax.broadcasted_iota(jnp.int32, (rows, KEY_BLOCK), 1)
            valid = jnp.logical_and(key_index >= low_ref[...], key_index < high_ref[...])
        for head in range(heads):
            cols = slice(head * HEAD_DIM, (head + 1) * HEAD_DIM)
            raw = lax.dot_general(
                query_ref[:, cols], key_ref[:, cols], (((1,), (1,)), ((), ())),
                preferred_element_type=jnp.float32,
            )
            old_max = max_ref[head]
            if masked:
                block_max = jnp.max(jnp.where(valid, raw, -1e30), axis=1, keepdims=True)
            else:
                block_max = jnp.max(raw, axis=1, keepdims=True)
            new_max = jnp.maximum(old_max, block_max)
            probs = jnp.exp2((raw - new_max) * EXP2_SCALE)
            if masked:
                probs = jnp.where(valid, probs, 0.0)
            alpha = jnp.exp2((old_max - new_max) * EXP2_SCALE)
            sum_ref[head] = alpha * sum_ref[head] + jnp.sum(probs, axis=1, keepdims=True)
            acc_ref[:, cols] = alpha * acc_ref[:, cols] + jnp.dot(
                probs.astype(jnp.bfloat16), value_ref[:, cols],
                preferred_element_type=jnp.float32,
            )
            max_ref[head] = new_max

    touched = jnp.logical_and(block >= first, block <= last)
    whole_block = jnp.logical_and(
        block * KEY_BLOCK >= span_ref[2], (block + 1) * KEY_BLOCK <= span_ref[3]
    )

    @pl.when(jnp.logical_and(touched, whole_block))
    def _():
        step(False)

    @pl.when(jnp.logical_and(touched, jnp.logical_not(whole_block)))
    def _():
        step(True)

    @pl.when(block == pl.num_programs(0) - 1)
    def _():
        for head in range(heads):
            cols = slice(head * HEAD_DIM, (head + 1) * HEAD_DIM)
            attended_ref[:, cols] = (acc_ref[:, cols] / sum_ref[head]).astype(jnp.bfloat16)
        own_ref[...] = jnp.dot(
            attended_ref[...], own_w_ref[...], preferred_element_type=jnp.float32
        )
        other_ref[...] = jnp.dot(
            attended_ref[...], other_w_ref[...], preferred_element_type=jnp.float32
        )


def attention(span, query, packed, query_low, query_high, own_w, other_w):
    rows, width = query.shape
    blocks = packed.shape[0] // KEY_BLOCK

    def key_map(block, span_ref):
        first = span_ref[0] // KEY_BLOCK
        last = (span_ref[1] - 1) // KEY_BLOCK
        return (jnp.minimum(jnp.maximum(block, first), last), 0)

    def value_map(block, span_ref):
        first = span_ref[0] // KEY_BLOCK
        last = (span_ref[1] - 1) // KEY_BLOCK
        return (jnp.minimum(jnp.maximum(block, first), last), 1)

    whole = lambda block, span_ref: (0, 0)
    heads = width // HEAD_DIM
    return pl.pallas_call(
        attention_kernel,
        grid_spec=pltpu.PrefetchScalarGridSpec(
            num_scalar_prefetch=1,
            grid=(blocks,),
            in_specs=[
                pl.BlockSpec((rows, width), whole),
                pl.BlockSpec((KEY_BLOCK, width), key_map),
                pl.BlockSpec((KEY_BLOCK, width), value_map),
                pl.BlockSpec((rows, 1), whole),
                pl.BlockSpec((rows, 1), whole),
                pl.BlockSpec(own_w.shape, whole),
                pl.BlockSpec(other_w.shape, whole),
            ],
            out_specs=[
                pl.BlockSpec((rows, own_w.shape[1]), whole),
                pl.BlockSpec((rows, other_w.shape[1]), whole),
            ],
            scratch_shapes=[
                pltpu.VMEM((heads, rows, 1), jnp.float32),
                pltpu.VMEM((heads, rows, 1), jnp.float32),
                pltpu.VMEM((rows, width), jnp.float32),
                pltpu.VMEM((rows, width), jnp.bfloat16),
            ],
        ),
        out_shape=(
            jax.ShapeDtypeStruct((rows, own_w.shape[1]), jnp.float32),
            jax.ShapeDtypeStruct((rows, other_w.shape[1]), jnp.float32),
        ),
    )(span, query, packed, packed, query_low, query_high, own_w, other_w)


def on_device(
    tokens, video_lengths, timestep, time_weight, block_mod, w_query, w_key, w_value, w_out
):
    tok_rows = tokens.shape[0]
    width = time_weight.shape[1] // 3
    first_core = lax.axis_index("tp") == 0
    other_half = lax.ppermute(tokens, "tp", perm=[(0, 1), (1, 0)])
    full_rows = jnp.where(
        first_core,
        jnp.concatenate([tokens, other_half], axis=1),
        jnp.concatenate([other_half, tokens], axis=1),
    )
    time_value = timestep[0].astype(jnp.float32)
    sigma = noise_level(time_value)
    delta_sigma = noise_level(time_value - 1.0) - sigma
    half_freq = time_weight.shape[0] // 2
    frequency = jnp.exp(-math.log(10000.0) * jnp.arange(half_freq, dtype=jnp.float32) / half_freq)
    angle = 1000.0 * sigma * frequency
    embedding = jnp.concatenate([jnp.cos(angle), jnp.sin(angle)])
    activated = jax.nn.silu(embedding)[:, None]
    shift_scale = jnp.sum(activated * time_weight[:, : 2 * width], axis=0).reshape(2, width)
    shift = shift_scale[0] + block_mod[0]
    scale = shift_scale[1] + block_mod[1]
    gate = jnp.sum(activated * time_weight[:, 2 * width :], axis=0) + block_mod[2]
    as_float = full_rows.astype(jnp.float32)
    mean = jnp.mean(as_float, axis=1, keepdims=True)
    centred = as_float - mean
    variance = jnp.mean(centred * centred, axis=1, keepdims=True)
    normed = (centred * lax.rsqrt(variance + 1e-06) * (1.0 + scale) + shift).astype(jnp.bfloat16)
    query = jnp.dot(normed, w_query, preferred_element_type=jnp.float32).astype(jnp.bfloat16)
    keys = jnp.dot(normed, w_key, preferred_element_type=jnp.float32).astype(jnp.bfloat16)
    values = jnp.dot(normed, w_value, preferred_element_type=jnp.float32).astype(jnp.bfloat16)
    start_row = lax.axis_index("req") * tok_rows
    query_index = start_row + jnp.arange(tok_rows, dtype=jnp.int32)
    video_ends = jnp.cumsum(video_lengths)
    video_starts = video_ends - video_lengths
    inside = jnp.logical_and(
        query_index[:, None] >= video_starts[None, :], query_index[:, None] < video_ends[None, :]
    )
    query_low = jnp.sum(jnp.where(inside, video_starts[None, :], 0), axis=1)
    query_high = jnp.sum(jnp.where(inside, video_ends[None, :], 0), axis=1)
    span = jnp.stack(
        [jnp.min(query_low), jnp.max(query_high), jnp.max(query_low), jnp.min(query_high)]
    ).astype(jnp.int32)
    packed = lax.all_gather(jnp.concatenate([keys, values], axis=1), "req", axis=0, tiled=True)
    share = w_out.shape[1] // 2
    core = lax.axis_index("tp")
    own_columns = lax.dynamic_slice_in_dim(w_out, core * share, share, axis=1)
    other_columns = lax.dynamic_slice_in_dim(w_out, (1 - core) * share, share, axis=1)
    own_part, other_part = attention(
        span, query, packed, query_low[:, None], query_high[:, None], own_columns, other_columns
    )
    partner_part = lax.ppermute(other_part, "tp", perm=[(0, 1), (1, 0)])
    projected = own_part + partner_part
    gate_share = lax.dynamic_slice_in_dim(gate, core * share, share)
    branch = gate_share[None, :] * projected
    velocity = branch.astype(jnp.bfloat16)
    stepped = (tokens.astype(jnp.float32) + delta_sigma * branch).astype(jnp.bfloat16)
    return (velocity, stepped)


def solution(mesh):
    return jax.shard_map(
        on_device,
        mesh=mesh,
        in_specs=(
            P("req", "tp"),
            P(),
            P(),
            P(),
            P(),
            P(None, "tp"),
            P(None, "tp"),
            P(None, "tp"),
            P("tp", None),
        ),
        out_specs=(P("req", "tp"), P("req", "tp")),
        check_vma=False,
    )
```

```python
import math

import jax
import jax.numpy as jnp
from jax import lax
from jax.experimental import pallas as pl
from jax.experimental.pallas import tpu as pltpu
from jax.sharding import PartitionSpec as P

HEAD_DIM = 128
STEPS = 1000
KEY_BLOCK = 2048
EXP2_SCALE = math.log2(math.e) / math.sqrt(HEAD_DIM)


def noise_level(step_value):
    frac = step_value / STEPS
    return 5.0 * frac / (1.0 + 4.0 * frac)


def attention_kernel(span_ref, query_ref, key_ref, value_ref, low_ref, high_ref, own_w_ref,
                     other_w_ref, own_ref, other_ref, max_ref, sum_ref, acc_ref, attended_ref):
    block = pl.program_id(0)
    heads = query_ref.shape[1] // HEAD_DIM
    first = span_ref[0] // KEY_BLOCK
    last = (span_ref[1] - 1) // KEY_BLOCK

    @pl.when(block == 0)
    def _():
        max_ref[...] = jnp.full(max_ref.shape, -1e30, jnp.float32)
        sum_ref[...] = jnp.zeros(sum_ref.shape, jnp.float32)
        acc_ref[...] = jnp.zeros(acc_ref.shape, jnp.float32)

    def step(masked):
        rows = query_ref.shape[0]
        if masked:
            key_index = block * KEY_BLOCK + lax.broadcasted_iota(jnp.int32, (rows, KEY_BLOCK), 1)
            valid = jnp.logical_and(key_index >= low_ref[...], key_index < high_ref[...])
        for head in range(heads):
            cols = slice(head * HEAD_DIM, (head + 1) * HEAD_DIM)
            raw = lax.dot_general(
                query_ref[:, cols], key_ref[:, cols], (((1,), (1,)), ((), ())),
                preferred_element_type=jnp.float32,
            )
            old_max = max_ref[head]
            if masked:
                block_max = jnp.max(jnp.where(valid, raw, -1e30), axis=1, keepdims=True)
            else:
                block_max = jnp.max(raw, axis=1, keepdims=True)
            new_max = jnp.maximum(old_max, block_max)
            probs = jnp.exp2((raw - new_max) * EXP2_SCALE)
            if masked:
                probs = jnp.where(valid, probs, 0.0)
            alpha = jnp.exp2((old_max - new_max) * EXP2_SCALE)
            sum_ref[head] = alpha * sum_ref[head] + jnp.sum(probs, axis=1, keepdims=True)
            acc_ref[:, cols] = alpha * acc_ref[:, cols] + jnp.dot(
                probs.astype(jnp.bfloat16), value_ref[:, cols],
                preferred_element_type=jnp.float32,
            )
            max_ref[head] = new_max

    touched = jnp.logical_and(block >= first, block <= last)
    whole_block = jnp.logical_and(
        block * KEY_BLOCK >= span_ref[2], (block + 1) * KEY_BLOCK <= span_ref[3]
    )

    @pl.when(jnp.logical_and(touched, whole_block))
    def _():
        step(False)

    @pl.when(jnp.logical_and(touched, jnp.logical_not(whole_block)))
    def _():
        step(True)

    @pl.when(block == pl.num_programs(0) - 1)
    def _():
        for head in range(heads):
            cols = slice(head * HEAD_DIM, (head + 1) * HEAD_DIM)
            attended_ref[:, cols] = (acc_ref[:, cols] / sum_ref[head]).astype(jnp.bfloat16)
        own_ref[...] = jnp.dot(
            attended_ref[...], own_w_ref[...], preferred_element_type=jnp.float32
        )
        other_ref[...] = jnp.dot(
            attended_ref[...], other_w_ref[...], preferred_element_type=jnp.float32
        )


def attention(span, query, packed, query_low, query_high, own_w, other_w):
    rows, width = query.shape
    blocks = packed.shape[0] // KEY_BLOCK

    def key_map(block, span_ref):
        first = span_ref[0] // KEY_BLOCK
        last = (span_ref[1] - 1) // KEY_BLOCK
        return (jnp.minimum(jnp.maximum(block, first), last), 0)

    def value_map(block, span_ref):
        first = span_ref[0] // KEY_BLOCK
        last = (span_ref[1] - 1) // KEY_BLOCK
        return (jnp.minimum(jnp.maximum(block, first), last), 1)

    whole = lambda block, span_ref: (0, 0)
    heads = width // HEAD_DIM
    return pl.pallas_call(
        attention_kernel,
        grid_spec=pltpu.PrefetchScalarGridSpec(
            num_scalar_prefetch=1,
            grid=(blocks,),
            in_specs=[
                pl.BlockSpec((rows, width), whole),
                pl.BlockSpec((KEY_BLOCK, width), key_map),
                pl.BlockSpec((KEY_BLOCK, width), value_map),
                pl.BlockSpec((rows, 1), whole),
                pl.BlockSpec((rows, 1), whole),
                pl.BlockSpec(own_w.shape, whole),
                pl.BlockSpec(other_w.shape, whole),
            ],
            out_specs=[
                pl.BlockSpec((rows, own_w.shape[1]), whole),
                pl.BlockSpec((rows, other_w.shape[1]), whole),
            ],
            scratch_shapes=[
                pltpu.VMEM((heads, rows, 1), jnp.float32),
                pltpu.VMEM((heads, rows, 1), jnp.float32),
                pltpu.VMEM((rows, width), jnp.float32),
                pltpu.VMEM((rows, width), jnp.bfloat16),
            ],
        ),
        out_shape=(
            jax.ShapeDtypeStruct((rows, own_w.shape[1]), jnp.float32),
            jax.ShapeDtypeStruct((rows, other_w.shape[1]), jnp.float32),
        ),
    )(span, query, packed, packed, query_low, query_high, own_w, other_w)


def on_device(
    tokens, video_lengths, timestep, time_weight, block_mod, w_query, w_key, w_value, w_out
):
    tok_rows = tokens.shape[0]
    width = time_weight.shape[1] // 3
    first_core = lax.axis_index("tp") == 0
    other_half = lax.ppermute(tokens, "tp", perm=[(0, 1), (1, 0)])
    full_rows = jnp.where(
        first_core,
        jnp.concatenate([tokens, other_half], axis=1),
        jnp.concatenate([other_half, tokens], axis=1),
    )
    time_value = timestep[0].astype(jnp.float32)
    sigma = noise_level(time_value)
    delta_sigma = noise_level(time_value - 1.0) - sigma
    half_freq = time_weight.shape[0] // 2
    frequency = jnp.exp(-math.log(10000.0) * jnp.arange(half_freq, dtype=jnp.float32) / half_freq)
    angle = 1000.0 * sigma * frequency
    embedding = jnp.concatenate([jnp.cos(angle), jnp.sin(angle)])
    activated = jax.nn.silu(embedding)[:, None]
    shift_scale = jnp.sum(activated * time_weight[:, : 2 * width], axis=0).reshape(2, width)
    shift = shift_scale[0] + block_mod[0]
    scale = shift_scale[1] + block_mod[1]
    gate = jnp.sum(activated * time_weight[:, 2 * width :], axis=0) + block_mod[2]
    as_float = full_rows.astype(jnp.float32)
    mean = jnp.mean(as_float, axis=1, keepdims=True)
    centred = as_float - mean
    variance = jnp.mean(centred * centred, axis=1, keepdims=True)
    normed = (centred * lax.rsqrt(variance + 1e-06) * (1.0 + scale) + shift).astype(jnp.bfloat16)
    query = jnp.dot(normed, w_query, preferred_element_type=jnp.float32).astype(jnp.bfloat16)
    keys = jnp.dot(normed, w_key, preferred_element_type=jnp.float32).astype(jnp.bfloat16)
    values = jnp.dot(normed, w_value, preferred_element_type=jnp.float32).astype(jnp.bfloat16)
    start_row = lax.axis_index("req") * tok_rows
    query_index = start_row + jnp.arange(tok_rows, dtype=jnp.int32)
    video_ends = jnp.cumsum(video_lengths)
    video_starts = video_ends - video_lengths
    inside = jnp.logical_and(
        query_index[:, None] >= video_starts[None, :], query_index[:, None] < video_ends[None, :]
    )
    query_low = jnp.sum(jnp.where(inside, video_starts[None, :], 0), axis=1)
    query_high = jnp.sum(jnp.where(inside, video_ends[None, :], 0), axis=1)
    span = jnp.stack(
        [jnp.min(query_low), jnp.max(query_high), jnp.max(query_low), jnp.min(query_high)]
    ).astype(jnp.int32)
    packed = lax.all_gather(jnp.concatenate([keys, values], axis=1), "req", axis=0, tiled=True)
    share = w_out.shape[1] // 2
    core = lax.axis_index("tp")
    own_columns = lax.dynamic_slice_in_dim(w_out, core * share, share, axis=1)
    other_columns = lax.dynamic_slice_in_dim(w_out, (1 - core) * share, share, axis=1)
    query, gate = lax.optimization_barrier((query, gate))
    own_part, other_part = attention(
        span, query, packed, query_low[:, None], query_high[:, None], own_columns, other_columns
    )
    partner_part = lax.ppermute(other_part, "tp", perm=[(0, 1), (1, 0)])
    projected = own_part + partner_part
    gate_share = lax.dynamic_slice_in_dim(gate, core * share, share)
    branch = gate_share[None, :] * projected
    velocity = branch.astype(jnp.bfloat16)
    stepped = (tokens.astype(jnp.float32) + delta_sigma * branch).astype(jnp.bfloat16)
    return (velocity, stepped)


def solution(mesh):
    return jax.shard_map(
        on_device,
        mesh=mesh,
        in_specs=(
            P("req", "tp"),
            P(),
            P(),
            P(),
            P(),
            P(None, "tp"),
            P(None, "tp"),
            P(None, "tp"),
            P("tp", None),
        ),
        out_specs=(P("req", "tp"), P("req", "tp")),
        check_vma=False,
    )
```

```python
import math

import jax
import jax.numpy as jnp
from jax import lax
from jax.experimental import pallas as pl
from jax.experimental.pallas import tpu as pltpu
from jax.sharding import PartitionSpec as P

HEAD_DIM = 128
STEPS = 1000
KEY_BLOCK = 2048
EXP2_SCALE = math.log2(math.e) / math.sqrt(HEAD_DIM)


def noise_level(step_value):
    frac = step_value / STEPS
    return 5.0 * frac / (1.0 + 4.0 * frac)


def attention_kernel(span_ref, query_ref, key_ref, value_ref, low_ref, high_ref, own_w_ref,
                     other_w_ref, own_ref, other_ref, max_ref, sum_ref, acc_ref, attended_ref):
    block = pl.program_id(0)
    heads = query_ref.shape[1] // HEAD_DIM
    first = span_ref[0] // KEY_BLOCK
    last = (span_ref[1] - 1) // KEY_BLOCK

    @pl.when(block == 0)
    def _():
        max_ref[...] = jnp.full(max_ref.shape, -1e30, jnp.float32)
        sum_ref[...] = jnp.zeros(sum_ref.shape, jnp.float32)
        acc_ref[...] = jnp.zeros(acc_ref.shape, jnp.float32)

    def step(masked, offset, size):
        rows = query_ref.shape[0]
        keys = pl.ds(offset, size)
        if masked:
            key_index = (
                block * KEY_BLOCK + offset + lax.broadcasted_iota(jnp.int32, (rows, size), 1)
            )
            valid = jnp.logical_and(key_index >= low_ref[...], key_index < high_ref[...])
        for head in range(heads):
            cols = slice(head * HEAD_DIM, (head + 1) * HEAD_DIM)
            raw = lax.dot_general(
                query_ref[:, cols], key_ref[keys, cols], (((1,), (1,)), ((), ())),
                preferred_element_type=jnp.float32,
            )
            old_max = max_ref[head]
            if masked:
                block_max = jnp.max(jnp.where(valid, raw, -1e30), axis=1, keepdims=True)
            else:
                block_max = jnp.max(raw, axis=1, keepdims=True)
            new_max = jnp.maximum(old_max, block_max)
            probs = jnp.exp2((raw - new_max) * EXP2_SCALE)
            if masked:
                probs = jnp.where(valid, probs, 0.0)
            alpha = jnp.exp2((old_max - new_max) * EXP2_SCALE)
            sum_ref[head] = alpha * sum_ref[head] + jnp.sum(probs, axis=1, keepdims=True)
            acc_ref[:, cols] = alpha * acc_ref[:, cols] + jnp.dot(
                probs.astype(jnp.bfloat16), value_ref[keys, cols],
                preferred_element_type=jnp.float32,
            )
            max_ref[head] = new_max

    half = KEY_BLOCK // 2
    base = block * KEY_BLOCK
    touched = jnp.logical_and(block >= first, block <= last)
    whole_block = jnp.logical_and(base >= span_ref[2], base + KEY_BLOCK <= span_ref[3])
    edge = jnp.logical_and(touched, jnp.logical_not(whole_block))
    need_low = jnp.logical_and(base < span_ref[1], base + half > span_ref[0])
    need_high = jnp.logical_and(base + half < span_ref[1], base + KEY_BLOCK > span_ref[0])

    @pl.when(jnp.logical_and(touched, whole_block))
    def _():
        step(False, 0, KEY_BLOCK)

    @pl.when(jnp.logical_and(edge, jnp.logical_and(need_low, need_high)))
    def _():
        step(True, 0, KEY_BLOCK)

    @pl.when(jnp.logical_and(edge, jnp.logical_and(need_low, jnp.logical_not(need_high))))
    def _():
        step(True, 0, half)

    @pl.when(jnp.logical_and(edge, jnp.logical_and(need_high, jnp.logical_not(need_low))))
    def _():
        step(True, half, half)

    @pl.when(block == pl.num_programs(0) - 1)
    def _():
        for head in range(heads):
            cols = slice(head * HEAD_DIM, (head + 1) * HEAD_DIM)
            attended_ref[:, cols] = (acc_ref[:, cols] / sum_ref[head]).astype(jnp.bfloat16)
        own_ref[...] = jnp.dot(
            attended_ref[...], own_w_ref[...], preferred_element_type=jnp.float32
        )
        other_ref[...] = jnp.dot(
            attended_ref[...], other_w_ref[...], preferred_element_type=jnp.float32
        )


def attention(span, query, packed, query_low, query_high, own_w, other_w):
    rows, width = query.shape
    blocks = packed.shape[0] // KEY_BLOCK

    def key_map(block, span_ref):
        first = span_ref[0] // KEY_BLOCK
        last = (span_ref[1] - 1) // KEY_BLOCK
        return (jnp.minimum(jnp.maximum(block, first), last), 0)

    def value_map(block, span_ref):
        first = span_ref[0] // KEY_BLOCK
        last = (span_ref[1] - 1) // KEY_BLOCK
        return (jnp.minimum(jnp.maximum(block, first), last), 1)

    whole = lambda block, span_ref: (0, 0)
    heads = width // HEAD_DIM
    return pl.pallas_call(
        attention_kernel,
        grid_spec=pltpu.PrefetchScalarGridSpec(
            num_scalar_prefetch=1,
            grid=(blocks,),
            in_specs=[
                pl.BlockSpec((rows, width), whole),
                pl.BlockSpec((KEY_BLOCK, width), key_map),
                pl.BlockSpec((KEY_BLOCK, width), value_map),
                pl.BlockSpec((rows, 1), whole),
                pl.BlockSpec((rows, 1), whole),
                pl.BlockSpec(own_w.shape, whole),
                pl.BlockSpec(other_w.shape, whole),
            ],
            out_specs=[
                pl.BlockSpec((rows, own_w.shape[1]), whole),
                pl.BlockSpec((rows, other_w.shape[1]), whole),
            ],
            scratch_shapes=[
                pltpu.VMEM((heads, rows, 1), jnp.float32),
                pltpu.VMEM((heads, rows, 1), jnp.float32),
                pltpu.VMEM((rows, width), jnp.float32),
                pltpu.VMEM((rows, width), jnp.bfloat16),
            ],
        ),
        out_shape=(
            jax.ShapeDtypeStruct((rows, own_w.shape[1]), jnp.float32),
            jax.ShapeDtypeStruct((rows, other_w.shape[1]), jnp.float32),
        ),
    )(span, query, packed, packed, query_low, query_high, own_w, other_w)


def on_device(
    tokens, video_lengths, timestep, time_weight, block_mod, w_query, w_key, w_value, w_out
):
    tok_rows = tokens.shape[0]
    width = time_weight.shape[1] // 3
    first_core = lax.axis_index("tp") == 0
    other_half = lax.ppermute(tokens, "tp", perm=[(0, 1), (1, 0)])
    full_rows = jnp.where(
        first_core,
        jnp.concatenate([tokens, other_half], axis=1),
        jnp.concatenate([other_half, tokens], axis=1),
    )
    time_value = timestep[0].astype(jnp.float32)
    sigma = noise_level(time_value)
    delta_sigma = noise_level(time_value - 1.0) - sigma
    half_freq = time_weight.shape[0] // 2
    frequency = jnp.exp(-math.log(10000.0) * jnp.arange(half_freq, dtype=jnp.float32) / half_freq)
    angle = 1000.0 * sigma * frequency
    embedding = jnp.concatenate([jnp.cos(angle), jnp.sin(angle)])
    activated = jax.nn.silu(embedding)[:, None]
    shift_scale = jnp.sum(activated * time_weight[:, : 2 * width], axis=0).reshape(2, width)
    shift = shift_scale[0] + block_mod[0]
    scale = shift_scale[1] + block_mod[1]
    gate = jnp.sum(activated * time_weight[:, 2 * width :], axis=0) + block_mod[2]
    as_float = full_rows.astype(jnp.float32)
    mean = jnp.mean(as_float, axis=1, keepdims=True)
    centred = as_float - mean
    variance = jnp.mean(centred * centred, axis=1, keepdims=True)
    normed = (centred * lax.rsqrt(variance + 1e-06) * (1.0 + scale) + shift).astype(jnp.bfloat16)
    query = jnp.dot(normed, w_query, preferred_element_type=jnp.float32).astype(jnp.bfloat16)
    keys = jnp.dot(normed, w_key, preferred_element_type=jnp.float32).astype(jnp.bfloat16)
    values = jnp.dot(normed, w_value, preferred_element_type=jnp.float32).astype(jnp.bfloat16)
    start_row = lax.axis_index("req") * tok_rows
    query_index = start_row + jnp.arange(tok_rows, dtype=jnp.int32)
    video_ends = jnp.cumsum(video_lengths)
    video_starts = video_ends - video_lengths
    inside = jnp.logical_and(
        query_index[:, None] >= video_starts[None, :], query_index[:, None] < video_ends[None, :]
    )
    query_low = jnp.sum(jnp.where(inside, video_starts[None, :], 0), axis=1)
    query_high = jnp.sum(jnp.where(inside, video_ends[None, :], 0), axis=1)
    span = jnp.stack(
        [jnp.min(query_low), jnp.max(query_high), jnp.max(query_low), jnp.min(query_high)]
    ).astype(jnp.int32)
    packed = lax.all_gather(jnp.concatenate([keys, values], axis=1), "req", axis=0, tiled=True)
    share = w_out.shape[1] // 2
    core = lax.axis_index("tp")
    own_columns = lax.dynamic_slice_in_dim(w_out, core * share, share, axis=1)
    other_columns = lax.dynamic_slice_in_dim(w_out, (1 - core) * share, share, axis=1)
    own_part, other_part = attention(
        span, query, packed, query_low[:, None], query_high[:, None], own_columns, other_columns
    )
    partner_part = lax.ppermute(other_part, "tp", perm=[(0, 1), (1, 0)])
    projected = own_part + partner_part
    gate_share = lax.dynamic_slice_in_dim(gate, core * share, share)
    branch = gate_share[None, :] * projected
    velocity = branch.astype(jnp.bfloat16)
    stepped = (tokens.astype(jnp.float32) + delta_sigma * branch).astype(jnp.bfloat16)
    return (velocity, stepped)


def solution(mesh):
    return jax.shard_map(
        on_device,
        mesh=mesh,
        in_specs=(
            P("req", "tp"),
            P(),
            P(),
            P(),
            P(),
            P(None, "tp"),
            P(None, "tp"),
            P(None, "tp"),
            P("tp", None),
        ),
        out_specs=(P("req", "tp"), P("req", "tp")),
        check_vma=False,
    )
```

```python
import math

import jax
import jax.numpy as jnp
from jax import lax
from jax.experimental import pallas as pl
from jax.experimental.pallas import tpu as pltpu
from jax.sharding import PartitionSpec as P

HEAD_DIM = 128
STEPS = 1000
KEY_BLOCK = 2048
EXP2_SCALE = math.log2(math.e) / math.sqrt(HEAD_DIM)


def noise_level(step_value):
    frac = step_value / STEPS
    return 5.0 * frac / (1.0 + 4.0 * frac)


def attention_kernel(span_ref, query_ref, key_ref, value_ref, low_ref, high_ref, other_w_ref,
                     own_ref, other_ref, max_ref, sum_ref, acc_ref):
    block = pl.program_id(0)
    heads = query_ref.shape[1] // HEAD_DIM
    first = span_ref[0] // KEY_BLOCK
    last = (span_ref[1] - 1) // KEY_BLOCK

    @pl.when(block == 0)
    def _():
        max_ref[...] = jnp.full(max_ref.shape, -1e30, jnp.float32)
        sum_ref[...] = jnp.zeros(sum_ref.shape, jnp.float32)
        acc_ref[...] = jnp.zeros(acc_ref.shape, jnp.float32)

    def step(masked):
        rows = query_ref.shape[0]
        if masked:
            key_index = block * KEY_BLOCK + lax.broadcasted_iota(jnp.int32, (rows, KEY_BLOCK), 1)
            valid = jnp.logical_and(key_index >= low_ref[...], key_index < high_ref[...])
        for head in range(heads):
            cols = slice(head * HEAD_DIM, (head + 1) * HEAD_DIM)
            raw = lax.dot_general(
                query_ref[:, cols], key_ref[:, cols], (((1,), (1,)), ((), ())),
                preferred_element_type=jnp.float32,
            )
            old_max = max_ref[head]
            if masked:
                block_max = jnp.max(jnp.where(valid, raw, -1e30), axis=1, keepdims=True)
            else:
                block_max = jnp.max(raw, axis=1, keepdims=True)
            new_max = jnp.maximum(old_max, block_max)
            probs = jnp.exp2((raw - new_max) * EXP2_SCALE)
            if masked:
                probs = jnp.where(valid, probs, 0.0)
            alpha = jnp.exp2((old_max - new_max) * EXP2_SCALE)
            sum_ref[head] = alpha * sum_ref[head] + jnp.sum(probs, axis=1, keepdims=True)
            acc_ref[:, cols] = alpha * acc_ref[:, cols] + jnp.dot(
                probs.astype(jnp.bfloat16), value_ref[:, cols],
                preferred_element_type=jnp.float32,
            )
            max_ref[head] = new_max

    touched = jnp.logical_and(block >= first, block <= last)
    whole_block = jnp.logical_and(
        block * KEY_BLOCK >= span_ref[2], (block + 1) * KEY_BLOCK <= span_ref[3]
    )

    @pl.when(jnp.logical_and(touched, whole_block))
    def _():
        step(False)

    @pl.when(jnp.logical_and(touched, jnp.logical_not(whole_block)))
    def _():
        step(True)

    @pl.when(block == pl.num_programs(0) - 1)
    def _():
        for head in range(heads):
            cols = slice(head * HEAD_DIM, (head + 1) * HEAD_DIM)
            own_ref[:, cols] = (acc_ref[:, cols] / sum_ref[head]).astype(jnp.bfloat16)
        other_ref[...] = jnp.dot(
            own_ref[...], other_w_ref[...], preferred_element_type=jnp.float32
        )


def attention(span, query, packed, query_low, query_high, other_w):
    rows, width = query.shape
    blocks = packed.shape[0] // KEY_BLOCK

    def key_map(block, span_ref):
        first = span_ref[0] // KEY_BLOCK
        last = (span_ref[1] - 1) // KEY_BLOCK
        return (jnp.minimum(jnp.maximum(block, first), last), 0)

    def value_map(block, span_ref):
        first = span_ref[0] // KEY_BLOCK
        last = (span_ref[1] - 1) // KEY_BLOCK
        return (jnp.minimum(jnp.maximum(block, first), last), 1)

    whole = lambda block, span_ref: (0, 0)
    heads = width // HEAD_DIM
    return pl.pallas_call(
        attention_kernel,
        grid_spec=pltpu.PrefetchScalarGridSpec(
            num_scalar_prefetch=1,
            grid=(blocks,),
            in_specs=[
                pl.BlockSpec((rows, width), whole),
                pl.BlockSpec((KEY_BLOCK, width), key_map),
                pl.BlockSpec((KEY_BLOCK, width), value_map),
                pl.BlockSpec((rows, 1), whole),
                pl.BlockSpec((rows, 1), whole),
                pl.BlockSpec(other_w.shape, whole),
            ],
            out_specs=[
                pl.BlockSpec((rows, width), whole),
                pl.BlockSpec((rows, other_w.shape[1]), whole),
            ],
            scratch_shapes=[
                pltpu.VMEM((heads, rows, 1), jnp.float32),
                pltpu.VMEM((heads, rows, 1), jnp.float32),
                pltpu.VMEM((rows, width), jnp.float32),
            ],
        ),
        out_shape=(
            jax.ShapeDtypeStruct((rows, width), jnp.bfloat16),
            jax.ShapeDtypeStruct((rows, other_w.shape[1]), jnp.float32),
        ),
    )(span, query, packed, packed, query_low, query_high, other_w)


def on_device(
    tokens, video_lengths, timestep, time_weight, block_mod, w_query, w_key, w_value, w_out
):
    tok_rows = tokens.shape[0]
    width = time_weight.shape[1] // 3
    first_core = lax.axis_index("tp") == 0
    other_half = lax.ppermute(tokens, "tp", perm=[(0, 1), (1, 0)])
    full_rows = jnp.where(
        first_core,
        jnp.concatenate([tokens, other_half], axis=1),
        jnp.concatenate([other_half, tokens], axis=1),
    )
    time_value = timestep[0].astype(jnp.float32)
    sigma = noise_level(time_value)
    delta_sigma = noise_level(time_value - 1.0) - sigma
    half_freq = time_weight.shape[0] // 2
    frequency = jnp.exp(-math.log(10000.0) * jnp.arange(half_freq, dtype=jnp.float32) / half_freq)
    angle = 1000.0 * sigma * frequency
    embedding = jnp.concatenate([jnp.cos(angle), jnp.sin(angle)])
    activated = jax.nn.silu(embedding)[:, None]
    shift_scale = jnp.sum(activated * time_weight[:, : 2 * width], axis=0).reshape(2, width)
    shift = shift_scale[0] + block_mod[0]
    scale = shift_scale[1] + block_mod[1]
    gate = jnp.sum(activated * time_weight[:, 2 * width :], axis=0) + block_mod[2]
    as_float = full_rows.astype(jnp.float32)
    mean = jnp.mean(as_float, axis=1, keepdims=True)
    centred = as_float - mean
    variance = jnp.mean(centred * centred, axis=1, keepdims=True)
    normed = (centred * lax.rsqrt(variance + 1e-06) * (1.0 + scale) + shift).astype(jnp.bfloat16)
    query = jnp.dot(normed, w_query, preferred_element_type=jnp.float32).astype(jnp.bfloat16)
    keys = jnp.dot(normed, w_key, preferred_element_type=jnp.float32).astype(jnp.bfloat16)
    values = jnp.dot(normed, w_value, preferred_element_type=jnp.float32).astype(jnp.bfloat16)
    start_row = lax.axis_index("req") * tok_rows
    query_index = start_row + jnp.arange(tok_rows, dtype=jnp.int32)
    video_ends = jnp.cumsum(video_lengths)
    video_starts = video_ends - video_lengths
    inside = jnp.logical_and(
        query_index[:, None] >= video_starts[None, :], query_index[:, None] < video_ends[None, :]
    )
    query_low = jnp.sum(jnp.where(inside, video_starts[None, :], 0), axis=1)
    query_high = jnp.sum(jnp.where(inside, video_ends[None, :], 0), axis=1)
    span = jnp.stack(
        [jnp.min(query_low), jnp.max(query_high), jnp.max(query_low), jnp.min(query_high)]
    ).astype(jnp.int32)
    packed = lax.all_gather(jnp.concatenate([keys, values], axis=1), "req", axis=0, tiled=True)
    share = w_out.shape[1] // 2
    core = lax.axis_index("tp")
    own_columns = lax.dynamic_slice_in_dim(w_out, core * share, share, axis=1)
    other_columns = lax.dynamic_slice_in_dim(w_out, (1 - core) * share, share, axis=1)
    query, gate = lax.optimization_barrier((query, gate))
    attended, other_part = attention(
        span, query, packed, query_low[:, None], query_high[:, None], other_columns
    )
    partner_part = lax.ppermute(other_part, "tp", perm=[(0, 1), (1, 0)])
    own_part = jnp.dot(attended, own_columns, preferred_element_type=jnp.float32)
    projected = own_part + partner_part
    gate_share = lax.dynamic_slice_in_dim(gate, core * share, share)
    branch = gate_share[None, :] * projected
    velocity = branch.astype(jnp.bfloat16)
    stepped = (tokens.astype(jnp.float32) + delta_sigma * branch).astype(jnp.bfloat16)
    return (velocity, stepped)


def solution(mesh):
    return jax.shard_map(
        on_device,
        mesh=mesh,
        in_specs=(
            P("req", "tp"),
            P(),
            P(),
            P(),
            P(),
            P(None, "tp"),
            P(None, "tp"),
            P(None, "tp"),
            P("tp", None),
        ),
        out_specs=(P("req", "tp"), P("req", "tp")),
        check_vma=False,
    )
```
